128 devices in a mesh: fem: 8 (over x, y_lo), bem: 16 (over y_hi, z, core).
Axes of the slice: x: 4, y: 4 (y_hi: 2, y_lo: 2; y = y_hi * 2 + y_lo), z: 4, core: 2. Of those that a mesh axis runs over, the one named last changes fastest.
Arguments:
- fem_field: float32 [64, 128, 32, 128], P('fem', 'bem'), may hold values from -6 to 6
- fem_source: float32 [64, 128, 32, 128], P('fem', 'bem'), may hold values from -6 to 6
- reaction: float32 [64, 128, 32], P('fem', 'bem'), may hold values from 0.5 to 3
- bem_density: float32 [128, 16384], P(None, 'bem'), may hold values from -6 to 6
- bem_source: float32 [128, 16384], P(None, 'bem'), may hold values from -6 to 6
- bem_diagonal: float32 [16384], P('bem'), may hold values from 2 to 6
- near_blocks: bfloat16 [32, 48, 512, 512], P('bem', 'fem'), may hold values from -0.0390625 to 0.0390625
- near_pairs: int32 [32, 48], P('bem'), may hold values from 0 to 31, as said below
- low_left: bfloat16 [32, 32, 512], P('bem'), may hold values from -1 to 1
- low_right: bfloat16 [32, 32, 512], replicated, may hold values from -0.25 to 0.25
- centers: float32 [32, 3], replicated, may hold values from 0 to 4
- trace_cell: int32 [32768], P(('fem', 'bem')), may hold values from 0 to 2047
- trace_bank: int32 [32768, 1], P(('fem', 'bem')), may hold values from 0 to 15; in each aligned block of 256 rows (0 to 255, 256 to 511, ...) at most 32 rows name the same one
- trace_row: int32 [32768], P(('fem', 'bem')), may hold values from 0 to 1023
Outputs:
- fem_out: float32 [64, 128, 32, 128], P('fem', 'bem')
- bem_out: float32 [128, 16384], P('fem', 'bem')
The draws below stay inside these ranges and needn't reach their ends.
Inputs may be any that keep to these rules, and one draw needn't show every extreme that they name: `trace_bank`: among the 256 slots of one device no bem index is named more than 32 times, and some device names some index exactly 32 times. Panel p's near-field source panels are held by bem indices within two of p's own, counted around the bem axis: near_pairs[p, k] // 2 - p // 2 is -2, -1, 0, 1 or 2 modulo 16.
All inputs are finite; a program needn't handle non-finite values.
Results may differ from the reference program's by a relative error of at most 0.0028.
Values may be sent and summed in bfloat16 or wider, within the bound.
No kernel may reach another device: no remote copies, remote signals or barrier semaphores. Data moves between devices by JAX's collectives and lax.ppermute only.
A program may use at most 128 MiB of HBM per device.

```python
import math
import jax
import jax.numpy as jnp
import numpy as np
from jax import lax

E = 128
CX = 8
CY = 8
CZ = 32
PANEL = 512
RANK = 32
NEAR = 48
PANEL_DEV = 2
TR_DEV = 256
CAP = 32
ITERS = 3
NX = 64
NY = 128
PANELS = 32
NB = 16384
SLOTS = 32768
N_FEM = 8
N_BEM = 16


def draw_near_pairs(key, part):
    home = jnp.arange(PANELS, dtype=jnp.int32)[:, None] // PANEL_DEV
    offset_bank = jax.random.randint(jax.random.fold_in(key, 11), (PANELS, NEAR), -2, 3)
    within = jax.random.randint(jax.random.fold_in(key, 12), (PANELS, NEAR), 0, PANEL_DEV)
    return ((home + offset_bank) % N_BEM * PANEL_DEV + within).astype(jnp.int32)


def with_ends(values, own_key, low, top_value):
    shape = values.shape
    place = [jax.random.randint(jax.random.fold_in(own_key, axis), (), 0, shape[axis]) for axis in range(len(shape))]
    values = values.at[tuple(place)].set(low)
    longest = shape.index(max(shape))
    place[longest] = (place[longest] + 1) % shape[longest]
    return values.at[tuple(place)].set(top_value)


def block_levels(rng, extent, cuts, least, high):
    def one(position, blocks):
        heights = jax.random.uniform(jax.random.fold_in(jax.random.fold_in(rng, 6), position), (blocks,), jnp.float32, least / len(cuts), high / len(cuts))
        return jnp.repeat(jnp.exp(heights), extent[position] // blocks).reshape((-1,) + (1,) * (len(extent) - position - 1))

    level = one(*cuts[0])
    for cut in cuts[1:]:
        level = level * one(*cut)
    return level


def shared_out(rng, own, number, rows, count, top, reach, skew):
    ranking = jax.random.permutation(rng, count)
    packed, ordinary = load_shares(count, rows * top, reach, skew, True), load_shares(count, rows * top, reach, skew, False)
    places = jnp.arange(count)

    def named(sizes, offset_by):
        used = int((sizes > 0).sum())
        fixed = max(1, used // 4)
        passed = fixed + (places - fixed + offset_by * (used - fixed)) % max(1, count - fixed)
        return jnp.zeros((count,), jnp.int32).at[ranking[jnp.where(places < fixed, places, passed)]].set(jnp.asarray(sizes, jnp.int32))

    sizes = jnp.where(number % 4 == 0, named(packed, number // 4), named(ordinary, number - number // 4 - 1))
    mixed = jax.random.permutation(jax.random.fold_in(own, 3), count)
    giver, sink = mixed[0:count // 2 * 2:2], mixed[1:count // 2 * 2:2]
    margin = jnp.minimum(sizes[giver] - 1, reach - sizes[sink]) // 2
    margin = jnp.where((giver == ranking[0]) | (sink == ranking[0]) | (sizes[sink] == 0), 0, jnp.maximum(margin, 0))
    passed = jax.random.randint(jax.random.fold_in(own, 4), (count // 2,), 0, 1 << 20) % (margin + 1)
    sizes = sizes.at[giver].add(-passed).at[sink].add(passed)
    labels = jnp.searchsorted(jnp.cumsum(sizes), jnp.arange(rows * top), side="right").astype(jnp.int32)
    table = labels.reshape(top, rows).T
    table = table[jax.random.permutation(jax.random.fold_in(own, 1), rows)]
    offset_by = jax.random.randint(jax.random.fold_in(own, 2), (rows, 1), 0, top)
    return jnp.take_along_axis(table, (jnp.arange(top)[None, :] + offset_by) % top, axis=1)


def load_shares(count, total, most, lean, full):
    weights = [(1 << 20) // math.isqrt(standing ** lean) + 1 for standing in range(1, count + 1)]
    largest = most if full else min(most, max(-(-total // count), total * weights[0] // sum(weights)))
    least = 1 if total - largest >= count - 1 else 0
    counts, rest = [largest] + [least] * (count - 1), total - largest - least * (count - 1)
    while rest > 0:
        candidates = [i for i in range(1, count) if counts[i] < largest] or [i for i in range(1, count) if counts[i] < most]
        mass, budget = sum([weights[i] for i in candidates]), rest
        for i in candidates:
            extra = min(most - counts[i], max(1, budget * weights[i] // mass), rest)
            counts[i] = counts[i] + extra
            rest = rest - extra
    return np.array(counts)


def gaussian(own_key, shape, spread, most, shards=(), kind=jnp.bfloat16):
    drawn = spread * jax.random.normal(own_key, shape, jnp.float32)
    if shards:
        drawn = drawn * block_levels(own_key, shape, shards, -0.22, 0.18)
    return jnp.clip(drawn, -most, most).astype(kind)


def setup_inputs(seed: int = 0) -> dict:
    seeds = jax.random.split(jax.random.key(seed), 15)
    fem_field = gaussian(seeds[0], (NX, NY, CZ, E), 1.0, 6.0, ((0, 8), (1, 16)), jnp.float32)
    fem_source = gaussian(seeds[1], (NX, NY, CZ, E), 1.0, 6.0, ((0, 8), (1, 16)), jnp.float32)
    reaction = jnp.clip(0.5 + 2.5 * jax.random.uniform(seeds[2], (NX, NY, CZ), jnp.float32) ** block_levels(seeds[2], (NX, NY, CZ), ((0, 8), (1, 16)), -0.2, 0.2), 0.5, 3.0)
    bem_density = gaussian(seeds[3], (E, NB), 1.0, 6.0, ((1, 16),), jnp.float32)
    bem_source = gaussian(seeds[4], (E, NB), 1.0, 6.0, ((1, 16),), jnp.float32)
    bem_diagonal = jnp.clip(jnp.exp(math.log(6.0) - 1.0986123 * jax.random.uniform(seeds[5], (NB,), jnp.float32) ** block_levels(seeds[5], (NB,), ((0, 16),), -0.2, 0.2)), 2.0, 6.0)
    near_blocks = gaussian(seeds[6], (PANELS, NEAR, PANEL, PANEL), (NEAR * PANEL) ** -0.5, 0.0390625, ((0, 16), (1, 8)))
    near_pairs = draw_near_pairs(jax.random.fold_in(seeds[14], 71), 0)
    low_left = gaussian(seeds[8], (PANELS, RANK, PANEL), RANK ** -0.5, 1.0, ((0, 16),))
    low_right = gaussian(seeds[9], (PANELS, RANK, PANEL), PANEL ** -0.5, 0.25)
    centers = jnp.clip(jax.random.uniform(seeds[10], (PANELS, 3), jnp.float32, 0.0, 4.0), 0.0, 4.0)
    trace_cell = with_ends(jax.random.randint(seeds[11], (SLOTS,), 0, CX * CY * CZ), jax.random.fold_in(seeds[11], 1), 0, (CX * CY * CZ) - 1).astype(jnp.int32)
    trace_bank_keys = jax.random.split(jax.random.fold_in(seeds[12], 1), SLOTS // TR_DEV)
    trace_bank_turns = jax.random.permutation(jax.random.fold_in(seeds[12], 3), SLOTS // TR_DEV)
    trace_bank = jax.vmap(lambda own, number: shared_out(jax.random.fold_in(seeds[12], 2), own, number, TR_DEV, N_BEM, 1, CAP, 2))(trace_bank_keys, trace_bank_turns).reshape((SLOTS, 1))
    trace_row = with_ends(jax.random.randint(seeds[13], (SLOTS,), 0, PANEL_DEV * PANEL), jax.random.fold_in(seeds[13], 1), 0, (PANEL_DEV * PANEL) - 1).astype(jnp.int32)
    return dict(fem_field=fem_field, fem_source=fem_source, reaction=reaction, bem_density=bem_density, bem_source=bem_source, bem_diagonal=bem_diagonal, near_blocks=near_blocks, near_pairs=near_pairs, low_left=low_left, low_right=low_right, centers=centers, trace_cell=trace_cell, trace_bank=trace_bank, trace_row=trace_row)


HIGHEST = lax.Precision.HIGHEST


def stiffness(state, reaction):
    padded = jnp.pad(state, ((1, 1), (1, 1), (1, 1), (0, 0)))
    beside = padded[2:, 1:-1, 1:-1] + padded[:-2, 1:-1, 1:-1]
    beside = beside + padded[1:-1, 2:, 1:-1] + padded[1:-1, :-2, 1:-1]
    beside = beside + padded[1:-1, 1:-1, 2:] + padded[1:-1, 1:-1, :-2]
    return (6.0 + reaction)[..., None] * state - beside


def by_device(state):
    blocks = state.reshape(N_FEM, CX, N_BEM, CY, CZ, E).transpose(0, 2, 1, 3, 4, 5)
    return blocks.reshape(N_FEM * N_BEM * CX * CY * CZ, E)


def from_device(flat):
    blocks = flat.reshape(N_FEM, N_BEM, CX, CY, CZ, E).transpose(0, 2, 1, 3, 4, 5)
    return blocks.reshape(N_FEM * CX, N_BEM * CY, CZ, E)


def near_field(rounded, near_blocks, near_pairs):
    grouped = rounded.reshape(E, PANELS, PANEL)

    def one_panel(pieces):
        blocks, pairs = pieces
        chosen = jnp.take(grouped, pairs, axis=1).astype(jnp.float32)
        return jnp.einsum("ekn,knm->em", chosen, blocks.astype(jnp.float32), precision=HIGHEST)

    rows = lax.map(one_panel, (near_blocks, near_pairs))
    return rows.transpose(1, 0, 2).reshape(E, PANELS * PANEL)


def far_field(rounded, low_left, low_right, centers, near_pairs):
    grouped = rounded.reshape(E, PANELS, PANEL).astype(jnp.float32)
    reduced = jnp.einsum("eqn,qrn->eqr", grouped, low_right.astype(jnp.float32), precision=HIGHEST).astype(jnp.bfloat16)
    reduced = lax.optimization_barrier(reduced).astype(jnp.float32)
    offsets = centers[:, None, :] - centers[None, :, :]
    kernel = 1.0 / (1.0 + jnp.sum(offsets * offsets, axis=-1))
    panel_ids = jnp.arange(PANELS, dtype=jnp.int32)
    listed = jnp.any(near_pairs[:, :, None] == panel_ids[None, None, :], axis=1)
    listed = listed | (panel_ids[:, None] == panel_ids[None, :])
    kernel = jnp.where(listed, 0.0, kernel)
    weights = jnp.einsum("pq,eqr->epr", kernel, reduced, precision=HIGHEST)
    distant = jnp.einsum("epr,prn->epn", weights, low_left.astype(jnp.float32), precision=HIGHEST)
    return distant.reshape(E, PANELS * PANEL)


def reference(fem_field, fem_source, reaction, bem_density, bem_source, bem_diagonal, near_blocks, near_pairs, low_left, low_right, centers, trace_cell, trace_bank, trace_row):
    slot_device = jnp.arange(trace_cell.shape[0], dtype=jnp.int32) // TR_DEV
    cell_index = (slot_device * (CX * CY * CZ) + trace_cell).astype(jnp.int32)
    node_index = (trace_bank[:, 0] * (PANEL_DEV * PANEL) + trace_row).astype(jnp.int32)
    fem_state = fem_field
    density = bem_density
    for sweep in range(ITERS):
        rounded = lax.optimization_barrier(density.astype(jnp.bfloat16))
        flat_fem = by_device(fem_state)
        traced = jnp.zeros((PANELS * PANEL, E), jnp.float32).at[node_index].add(flat_fem[cell_index])
        applied = near_field(rounded, near_blocks, near_pairs) + far_field(rounded, low_left, low_right, centers, near_pairs) + traced.T
        coupled_flat = jnp.zeros((N_FEM * N_BEM * CX * CY * CZ, E), jnp.float32).at[cell_index].add(density.T[node_index])
        coupled = from_device(coupled_flat)
        fem_next = fem_state + (fem_source - stiffness(fem_state, reaction) - coupled) / (6.0 + reaction)[..., None]
        density = density + (bem_source - applied) / bem_diagonal[None, :]
        fem_state = fem_next
    return fem_state, density
```

```python
import jax
import jax.numpy as jnp
from jax import lax
from jax.experimental import pallas as pl
from jax.experimental.pallas import tpu as pltpu
from jax.sharding import PartitionSpec as P

CAP = 32
ITERS = 3
HIGHEST = lax.Precision.HIGHEST
BF16 = jnp.bfloat16
F32 = jnp.float32


def matmul(left, right, dims):
    return lax.dot_general(left, right, (dims, ((), ())), preferred_element_type=F32)


def near_kernel(table, *refs):
    blocks, received, hot, weights, factors, out, panels, total = refs[6:]
    step = pl.program_id(0)
    rows = total.shape[2]
    per_dev = total.shape[0]
    share = received.shape[1] - CAP

    @pl.when(step == 0)
    def start():
        for place, ref in enumerate(refs[:6]):
            for half in range(per_dev):
                panels[place * per_dev + half] = ref[:, half * rows : (half + 1) * rows]
        values = received[:, :CAP, :].reshape(-1, received.shape[2])
        traced = matmul(values, hot[...], ((0,), (0,)))
        first = pl.multiple_of(table[table.shape[0] - 1], share)
        for half in range(per_dev):
            total[half] = traced[:, half * rows : (half + 1) * rows]
            mixed = jnp.zeros((share, received.shape[2]), F32)
            for bank in range(received.shape[0]):
                mixed = mixed + weights[bank, half : half + 1, :] * received[bank, CAP:, :].astype(
                    F32
                )
            upper = mixed.astype(BF16)
            lower = (mixed - upper.astype(F32)).astype(BF16)
            far = matmul(upper, factors[half], ((1,), (0,))) + matmul(
                lower, factors[half], ((1,), (0,))
            )
            total[half, pl.ds(first, share), :] += far

    for half in range(per_dev):
        place = table[half * pl.num_programs(0) + step]
        total[half] += matmul(panels[place], blocks[half, 0], ((1,), (0,)))

    @pl.when(step == pl.num_programs(0) - 1)
    def finish():
        for half in range(per_dev):
            out[:, half * rows : (half + 1) * rows] = total[half].astype(BF16)


def near_call(table, parts, near_blocks, received, hot, weights, factors):
    per_dev, group, rows, _ = near_blocks.shape
    excitations = parts[0].shape[0]

    def whole(x):
        return pl.BlockSpec(x.shape, lambda *_: (0,) * x.ndim, pipeline_mode=pl.Buffered(1))

    return pl.pallas_call(
        near_kernel,
        out_shape=jax.ShapeDtypeStruct((excitations, per_dev * rows), BF16),
        grid_spec=pltpu.PrefetchScalarGridSpec(
            num_scalar_prefetch=1,
            grid=(group,),
            in_specs=[whole(x) for x in parts]
            + [pl.BlockSpec((per_dev, 1, rows, rows), lambda k, _: (0, k, 0, 0))]
            + [whole(x) for x in (received, hot, weights, factors)],
            out_specs=pl.BlockSpec((excitations, per_dev * rows), lambda k, _: (0, 0)),
            scratch_shapes=[
                pltpu.VMEM((6 * per_dev, excitations, rows), BF16),
                pltpu.VMEM((per_dev, excitations, rows), F32),
            ],
        ),
        compiler_params=pltpu.CompilerParams(vmem_limit_bytes=24 << 20),
        cost_estimate=pl.CostEstimate(
            flops=2 * excitations * per_dev * group * rows * rows,
            bytes_accessed=2 * per_dev * group * rows * rows,
            transcendentals=0,
        ),
        name="near",
    )(table, *parts, near_blocks, received, hot, weights, factors)


def fem_kernel(state, source, inverse, spread, returned, low0, high0, low1, high1, *refs):
    out, padded, coupled = refs[0], refs[-2], refs[-1]
    cx, cy, cz, lanes = state.shape
    coupled[...] = matmul(spread[...], returned[...], ((1,), (0,)))
    padded[0, 1 : cy + 1] = low0[...].astype(F32)
    padded[cx + 1, 1 : cy + 1] = high0[...].astype(F32)
    for i in range(cx):
        padded[i + 1, 0] = low1[i].astype(F32)
        padded[i + 1, 1 : cy + 1] = state[i]
        padded[i + 1, cy + 1] = high1[i].astype(F32)
    depth = lax.broadcasted_iota(jnp.int32, (cz, lanes), 0)

    def plane(m, carry):
        i, j = m // cy, m % cy
        here = padded[i + 1, j + 1]
        beside = padded[i + 2, j + 1] + padded[i, j + 1]
        beside = beside + padded[i + 1, j + 2] + padded[i + 1, j]
        beside = beside + jnp.where(depth == cz - 1, 0.0, pltpu.roll(here, cz - 1, 0))
        beside = beside + jnp.where(depth == 0, 0.0, pltpu.roll(here, 1, 0))
        first = pl.multiple_of(m * cz, cz)
        value = source[i, j] + beside - coupled[pl.ds(first, cz), :]
        out[i, j] = value * inverse[i, j]
        return carry

    lax.fori_loop(0, cx * cy, plane, 0, unroll=4)
    if len(refs) > 3:
        take = refs[1]
        values, edge0l, edge0h, edge1l, edge1h = refs[2:7]
        narrow = out[...].reshape(cx * cy * cz, lanes).astype(BF16)
        values[...] = matmul(take[...], narrow, ((1,), (0,))).astype(BF16)
        edge0l[...] = out[0].astype(BF16)
        edge0h[...] = out[cx - 1].astype(BF16)
        for i in range(cx):
            edge1l[i] = out[i, 0].astype(BF16)
            edge1h[i] = out[i, cy - 1].astype(BF16)


def fem_body_last(*refs):
    fem_kernel(*refs)


def fem_body(*refs):
    fem_kernel(*refs[:9], refs[10], refs[9], *refs[11:])


def fem_call(state, source, inverse, spread, returned, halos, take, last):
    cx, cy, cz, lanes = state.shape
    outs = [jax.ShapeDtypeStruct(state.shape, F32)]
    ins = [state, source, inverse, spread, returned, *halos]
    if not last:
        ins.append(take)
        outs.append(jax.ShapeDtypeStruct((take.shape[0], lanes), BF16))
        outs += [jax.ShapeDtypeStruct((cy, cz, lanes), BF16)] * 2
        outs += [jax.ShapeDtypeStruct((cx, cz, lanes), BF16)] * 2
    vmem = pl.BlockSpec(memory_space=pltpu.VMEM)
    return pl.pallas_call(
        fem_body_last if last else fem_body,
        out_shape=outs,
        in_specs=[vmem] * len(ins),
        out_specs=[vmem] * len(outs),
        scratch_shapes=[
            pltpu.VMEM((cx + 2, cy + 2, cz, lanes), F32),
            pltpu.VMEM((cx * cy * cz, lanes), F32),
        ],
        compiler_params=pltpu.CompilerParams(vmem_limit_bytes=32 << 20),
        cost_estimate=pl.CostEstimate(
            flops=4 * spread.size * lanes, bytes_accessed=8 << 20, transcendentals=0
        ),
        name="fem_last" if last else "fem_step",
    )(*ins)


def exchange(x, axis):
    return lax.all_to_all(x, axis, split_axis=0, concat_axis=0, tiled=True)


def along(x, axis, shift):
    size = lax.axis_size(axis)
    pairs = [(i, i + shift) for i in range(size) if 0 <= i + shift < size]
    return lax.ppermute(x, axis, pairs)


def around(x, axis, shift):
    size = lax.axis_size(axis)
    return lax.ppermute(x, axis, [(i, (i + shift) % size) for i in range(size)])


def partner(x, axis):
    return lax.ppermute(x, axis, [(i, i ^ 1) for i in range(lax.axis_size(axis))])


def shards(
    fem_field,
    fem_source,
    reaction,
    bem_density,
    bem_source,
    bem_diagonal,
    near_blocks,
    near_pairs,
    low_left,
    low_right,
    centers,
    trace_cell,
    trace_bank,
    trace_row,
):
    fem_count = lax.axis_size("fem")
    bem_count = lax.axis_size("bem")
    fem_rank = lax.axis_index("fem")
    bem_rank = lax.axis_index("bem")
    excitations, local_rows = bem_density.shape
    share = excitations // fem_count
    per_dev, group, panel_rows, _ = near_blocks.shape
    panel_total, rank, _ = low_right.shape
    cells = reaction.size
    slots = trace_cell.shape[0]
    places = bem_count * CAP
    first_col = fem_rank * share
    own_first = bem_rank * per_dev

    bank = trace_bank[:, 0]
    order = jnp.arange(slots, dtype=jnp.int32)
    earlier = (bank[:, None] == bank[None, :]) & (order[:, None] < order[None, :])
    place = bank * CAP + jnp.sum(earlier.astype(jnp.int32), axis=0)
    hit = jnp.arange(places, dtype=jnp.int32)[:, None] == place[None, :]
    row_code = jnp.sum(jnp.where(hit, trace_row[None, :] + 1, 0), axis=1)
    cell_code = jnp.sum(jnp.where(hit, trace_cell[None, :] + 1, 0), axis=1)
    cell_ids = jnp.arange(1, cells + 1, dtype=jnp.int32)
    take = (cell_code[:, None] == cell_ids[None, :]).astype(BF16)
    spread = (cell_ids[:, None] == cell_code[None, :]).astype(BF16)

    own_centers = lax.dynamic_slice_in_dim(centers, own_first, per_dev, 0)
    offsets = own_centers[:, None, :] - centers[None, :, :]
    kernel_rows = 1.0 / (1.0 + jnp.sum(offsets * offsets, axis=-1))
    panel_ids = jnp.arange(panel_total, dtype=jnp.int32)
    own_ids = own_first + jnp.arange(per_dev, dtype=jnp.int32)
    listed = jnp.any(near_pairs[:, :, None] == panel_ids[None, None, :], axis=1)
    listed = listed | (own_ids[:, None] == panel_ids[None, :])
    kernel_rows = jnp.where(listed, 0.0, kernel_rows)
    weights = jnp.repeat(kernel_rows.reshape(per_dev, bem_count, per_dev), rank, axis=2)
    weights = jnp.pad(weights.transpose(1, 0, 2), ((0, 0), (0, 0), (0, 128 - per_dev * rank)))
    factors = jnp.concatenate([low_left] * per_dev, axis=1)
    factors = jnp.pad(factors, ((0, 0), (0, 128 - per_dev * rank), (0, 0)))
    own_right = lax.dynamic_slice_in_dim(low_right, own_first, per_dev, 0)

    sources = lax.dynamic_slice_in_dim(near_pairs, fem_rank * group, group, 1)
    source_bank = sources // per_dev
    chip = jnp.mod(source_bank // 2 - bem_rank // 2 + 1, bem_count // 2)
    other = (source_bank + bem_rank) % 2
    table = ((chip * 2 + other) * per_dev + sources % per_dev).reshape(-1)
    table = jnp.concatenate([table, first_col[None]]).astype(jnp.int32)

    inverse = jnp.broadcast_to((1.0 / (6.0 + reaction))[..., None], fem_field.shape)
    density = lax.dynamic_slice_in_dim(bem_density, first_col, share, 0)
    source_part = lax.dynamic_slice_in_dim(bem_source, first_col, share, 0)
    diag_row = bem_diagonal[None, :]

    def moments(narrow):
        grouped = narrow.reshape(share, per_dev, panel_rows)
        reduced = jnp.einsum("eqn,qrn->eqr", grouped, own_right, preferred_element_type=F32)
        return reduced.astype(BF16).reshape(share, per_dev * rank)

    narrow = density.astype(BF16)
    full = bem_density.astype(BF16)
    fem_state = fem_field
    edges = (fem_field[0], fem_field[-1], fem_field[:, 0], fem_field[:, -1])
    edges = [x.astype(BF16) for x in edges]
    values = matmul(take, fem_field.reshape(cells, excitations).astype(BF16), ((1,), (0,)))
    values = values.astype(BF16)
    digits = jnp.stack([row_code // 32, row_code % 32]).reshape(2, bem_count, CAP)
    digits = digits.transpose(1, 0, 2).reshape(bem_count, 1, 2 * CAP).astype(BF16)
    digits = jnp.pad(digits, ((0, 0), (0, share - 1), (0, 0)))
    hot = None
    for sweep in range(ITERS):
        if sweep > 0:
            copies = jnp.broadcast_to(narrow, (fem_count, share, local_rows))
            full = exchange(copies, "fem").reshape(excitations, local_rows)
        far = jnp.broadcast_to(moments(narrow), (bem_count, share, per_dev * rank))
        tail = digits if sweep == 0 else jnp.zeros_like(digits)
        far = jnp.concatenate([far, tail], axis=2)
        sent = jnp.concatenate([values.reshape(bem_count, CAP, excitations), far], axis=1)
        received = exchange(sent, "bem")
        if hot is None:
            coded = received[:, CAP, 2 * CAP :].astype(F32)
            rows = (coded[:, :CAP] * 32.0 + coded[:, CAP:]).astype(jnp.int32).reshape(-1)
            hot = (rows[:, None] == jnp.arange(1, local_rows + 1, dtype=jnp.int32)).astype(BF16)
        left = around(full, "bem", 2)
        right = around(full, "bem", -2)
        parts = [
            left,
            partner(left, "bem"),
            full,
            partner(full, "bem"),
            right,
            partner(right, "bem"),
        ]
        picked = matmul(hot, full, ((1,), (1,))).astype(BF16)
        returned = exchange(picked.reshape(bem_count, CAP, excitations), "bem")
        low0 = along(edges[1], "fem", 1)
        high0 = along(edges[0], "fem", -1)
        low1 = along(edges[3], "bem", 1)
        high1 = along(edges[2], "bem", -1)
        partial = near_call(table, parts, near_blocks, received, hot, weights, factors)
        summed = exchange(partial.reshape(fem_count, share, local_rows), "fem")
        applied = summed.astype(F32).sum(axis=0)
        last = sweep == ITERS - 1
        fem_state, *rest = fem_call(
            fem_state,
            fem_source,
            inverse,
            spread,
            returned.reshape(places, excitations),
            (low0, high0, low1, high1),
            take,
            last,
        )
        density = density + (source_part - applied) / diag_row
        if not last:
            narrow = density.astype(BF16)
            values, *edges = rest
    return (fem_state, density)


def solution(mesh):
    return jax.shard_map(
        shards,
        mesh=mesh,
        in_specs=(
            P("fem", "bem", None, None),
            P("fem", "bem", None, None),
            P("fem", "bem", None),
            P(None, "bem"),
            P(None, "bem"),
            P("bem"),
            P("bem", "fem", None, None),
            P("bem", None),
            P("bem", None, None),
            P(),
            P(),
            P(("fem", "bem")),
            P(("fem", "bem"), None),
            P(("fem", "bem")),
        ),
        out_specs=(P("fem", "bem", None, None), P("fem", "bem")),
        check_vma=False,
    )
```

```python
import functools

import jax
import jax.numpy as jnp
from jax import lax
from jax.experimental import pallas as pl
from jax.experimental.pallas import tpu as pltpu
from jax.sharding import PartitionSpec as P

CAP = 32
ITERS = 3
HIGHEST = lax.Precision.HIGHEST
BF16 = jnp.bfloat16
F32 = jnp.float32


def matmul(left, right, dims):
    return lax.dot_general(left, right, (dims, ((), ())), preferred_element_type=F32)


def kernel_call(body, args, outs, scratch, copies, flops, name, smem=()):
    hbm = pl.BlockSpec(memory_space=pltpu.HBM)
    scalar = pl.BlockSpec(memory_space=pltpu.SMEM)
    args = [*smem, *args]
    return pl.pallas_call(
        body,
        out_shape=outs,
        in_specs=[scalar] * len(smem) + [hbm] * (len(args) - len(smem)),
        out_specs=[hbm] * len(outs),
        scratch_shapes=[pltpu.VMEM(s, t) for s, t in scratch] + [pltpu.SemaphoreType.DMA((copies,))],
        compiler_params=pltpu.CompilerParams(vmem_limit_bytes=64 << 20),
        cost_estimate=pl.CostEstimate(
            flops=flops,
            bytes_accessed=sum(x.size * x.dtype.itemsize for x in args),
            transcendentals=0,
        ),
        name=name,
    )(*args)


class Copies:
    def __init__(self, sems):
        self.sems, self.count = sems, 0

    def start(self, source, target):
        copy = pltpu.make_async_copy(source, target, self.sems.at[self.count])
        self.count += 1
        copy.start()
        return copy


def near_body(table, *refs):
    parts = refs[:6]
    blocks, received, hot, weights, factors, out = refs[6:12]
    panels, held, got, mask, mix, factor, total, narrow, sems = refs[12:]
    per_dev, group, rows, _ = blocks.shape
    share = panels.shape[1] // 8
    copies = Copies(sems)
    small = [
        copies.start(received, got),
        copies.start(hot, mask),
        copies.start(weights, mix),
        copies.start(factors, factor),
    ]
    moved = []
    for place, ref in enumerate(parts):
        for half in range(per_dev):
            moved.append(
                copies.start(
                    ref.at[:, half * rows : (half + 1) * rows], panels.at[place * per_dev + half]
                )
            )
    loads = []
    for half in range(per_dev):
        for step in range(group):
            loads.append(copies.start(blocks.at[half, step], held.at[half * group + step]))
    for copy in small:
        copy.wait()
    values = got[:, :CAP, :].reshape(-1, got.shape[2])
    traced = matmul(values, mask[...], ((0,), (0,)))
    first = pl.multiple_of(table[table.shape[0] - 1], share)
    for half in range(per_dev):
        total[half] = traced[:, half * rows : (half + 1) * rows]
        mixed = jnp.zeros((share, got.shape[2]), F32)
        for bank in range(got.shape[0]):
            mixed = mixed + mix[bank, half : half + 1, :] * got[
                bank, got.shape[1] - share :, :
            ].astype(F32)
        upper = mixed.astype(BF16)
        lower = (mixed - upper.astype(F32)).astype(BF16)
        far = matmul(upper, factor[half], ((1,), (0,))) + matmul(lower, factor[half], ((1,), (0,)))
        total[half, pl.ds(first, share), :] += far
    for copy in moved:
        copy.wait()
    done = []
    for half in range(per_dev):
        summed = total[half]
        for step in range(group):
            loads[half * group + step].wait()
            place = table[half * group + step]
            summed = summed + matmul(panels[place], held[half * group + step], ((1,), (0,)))
        narrow[half] = summed.astype(BF16)
        done.append(copies.start(narrow.at[half], out.at[:, half * rows : (half + 1) * rows]))
    for copy in done:
        copy.wait()


def near_call(table, parts, near_blocks, received, hot, weights, factors):
    per_dev, group, rows, _ = near_blocks.shape
    excitations = parts[0].shape[0]
    (out,) = kernel_call(
        near_body,
        [*parts, near_blocks, received, hot, weights, factors],
        [jax.ShapeDtypeStruct((excitations, per_dev * rows), BF16)],
        [
            ((6 * per_dev, excitations, rows), BF16),
            ((per_dev * group, rows, rows), BF16),
            (received.shape, BF16),
            (hot.shape, BF16),
            (weights.shape, F32),
            (factors.shape, BF16),
            ((per_dev, excitations, rows), F32),
            ((per_dev, excitations, rows), BF16),
        ],
        4 + 6 * per_dev + per_dev * group + per_dev,
        2 * excitations * near_blocks.size // rows * rows,
        "near",
        smem=[table],
    )
    return out


def write_edges(state, take, values, edges, chosen, rims, parity, copies):
    cx, cy, cz, lanes = state.shape
    rims[0] = state[0].astype(BF16)
    rims[1] = state[cx - 1].astype(BF16)
    for i in range(cx):
        rims[2, i] = state[i, 0].astype(BF16)
        rims[3, i] = state[i, cy - 1].astype(BF16)
    done = [copies.start(rims.at[place], edges[k]) for k, place in enumerate(rim_places(parity))]
    narrow = state[...].reshape(cx * cy * cz, lanes).astype(BF16)
    chosen[...] = matmul(take[...], narrow, ((1,), (0,))).astype(BF16)
    if values is not None:
        done.append(copies.start(chosen, values))
    return done


def rim_places(parity):
    return (1 - parity[0], parity[0], 3 - parity[1], 2 + parity[1])


def setup_body(parity, first, *refs):
    bank, cell, row, state, density, right = refs[:6]
    sent, take, codes = refs[6:9]
    edges = refs[9:13]
    banks_v, cells_v, rows_v, here, share_v, factor, packed, picks, coded, chosen, rims, sems = refs[
        13:
    ]
    copies = Copies(sems)
    small = [copies.start(bank, banks_v), copies.start(cell, cells_v), copies.start(row, rows_v)]
    share = share_v.shape[0]
    start = pl.multiple_of(first[0], share)
    large = [
        copies.start(density.at[pl.ds(start, share)], share_v),
        copies.start(right.at[pl.ds(first[1], factor.shape[0])], factor),
        copies.start(state, here),
    ]
    for copy in small:
        copy.wait()
    slots, banks, lanes = bank.shape[1], sent.shape[0], sent.shape[2]
    places, cells = take.shape
    down = lax.broadcasted_iota(jnp.int32, (slots, slots), 0)
    over = lax.broadcasted_iota(jnp.int32, (slots, slots), 1)

    def column(x):
        return jnp.sum(jnp.where(down == over, x, 0), axis=1, keepdims=True)

    bank_r, cell_r, code_r = banks_v[...], cells_v[...] + 1, rows_v[...] + 1
    bank_c = column(bank_r)
    same = bank_c == bank_r
    place_r = bank_r * CAP + jnp.sum(
        jnp.where(same & (down < over), 1, 0), axis=0, keepdims=True
    )
    within_c = jnp.sum(jnp.where(same & (over < down), 1, 0), axis=1, keepdims=True)
    place_c = bank_c * CAP + within_c
    hit = lax.broadcasted_iota(jnp.int32, (places, slots), 0) == place_r
    cell_c = jnp.sum(jnp.where(hit, cell_r, 0), axis=1, keepdims=True)
    ids = lax.broadcasted_iota(jnp.int32, (places, cells), 1) + 1
    picks[...] = (cell_c == ids).astype(F32).astype(BF16)
    out = [copies.start(picks, take)]
    hit = lax.broadcasted_iota(jnp.int32, (slots, places), 1) == place_c
    coded[...] = jnp.sum(jnp.where(hit, column(cell_r), 0), axis=0, keepdims=True)
    out.append(copies.start(coded, codes))
    lane = lax.broadcasted_iota(jnp.int32, (slots, lanes), 1)
    named = lax.broadcasted_iota(jnp.int32, (banks, slots), 0) == bank_r
    digits = jnp.zeros((banks, lanes), F32)
    for digit, base in ((code_r // 32, lanes - 2 * CAP), (code_r % 32, lanes - CAP)):
        mine = jnp.where(named, digit, 0).astype(F32).astype(BF16)
        where = (lane == within_c + base).astype(F32).astype(BF16)
        digits = digits + matmul(mine, where, ((1,), (0,)))
    for copy in large:
        copy.wait()
    out += write_edges(here, picks, None, edges, chosen, rims, parity, copies)
    moment = moments(share_v[...].astype(BF16), factor)
    top = lax.broadcasted_iota(jnp.int32, moment.shape, 0) == 0
    packed[:, :CAP] = chosen[...].reshape(banks, CAP, lanes)
    for k in range(banks):
        packed[k, CAP:] = (moment + jnp.where(top, digits[k : k + 1], 0.0)).astype(BF16)
    out.append(copies.start(packed, sent))
    for copy in out:
        copy.wait()


def moments(rounded, factor):
    per_dev, rank, rows = factor.shape
    sums = [
        matmul(rounded[:, q * rows : (q + 1) * rows], factor[q], ((1,), (1,)))
        for q in range(per_dev)
    ]
    sums.append(jnp.zeros((rounded.shape[0], 128 - per_dev * rank), F32))
    return jnp.concatenate(sums, axis=1)


def setup_call(parity, first, bank, cell, row, state, density, right, banks, share, per_dev):
    cx, cy, cz, lanes = state.shape
    slots = bank.shape[1]
    take = jax.ShapeDtypeStruct((banks * CAP, cx * cy * cz), BF16)
    return kernel_call(
        setup_body,
        [bank, cell, row, state, density, right],
        [
            jax.ShapeDtypeStruct((banks, CAP + share, lanes), BF16),
            take,
            jax.ShapeDtypeStruct((1, banks * CAP), jnp.int32),
        ]
        + edge_shapes(state),
        [
            ((1, slots), jnp.int32),
            ((1, slots), jnp.int32),
            ((1, slots), jnp.int32),
            (state.shape, F32),
            ((share, density.shape[1]), F32),
            ((per_dev, *right.shape[1:]), BF16),
            ((banks, CAP + share, lanes), BF16),
            (take.shape, BF16),
            ((1, banks * CAP), jnp.int32),
            ((banks * CAP, lanes), BF16),
            ((4, cx, cz, lanes), BF16),
        ],
        13,
        2 * take.size * lanes,
        "setup",
        smem=[parity, first],
    )


def edge_shapes(state):
    cx, cy, cz, lanes = state.shape
    return [jax.ShapeDtypeStruct((cx, cz, lanes), BF16)] * 4


def fem_body(last, parity, *refs):
    state, source, inverse, spread, returned = refs[:5]
    halos = refs[5:9]
    if last:
        out = refs[9]
        padded, load, scale, wide, back, rim, coupled, fresh, sems = refs[10:]
    else:
        take, out, values = refs[9:12]
        edges = refs[12:16]
        padded, load, scale, wide, back, rim, coupled, fresh = refs[16:24]
        picks, chosen, rims, sems = refs[24:]
    cx, cy, cz, lanes = state.shape
    first_row = 0 if returned.shape[1] == CAP else CAP
    copies = Copies(sems)
    early = [
        copies.start(spread, wide),
        copies.start(returned.at[:, first_row : first_row + CAP], back),
    ]
    early_b = [
        copies.start(halos[k], rim.at[place]) for k, place in enumerate(rim_places(parity))
    ]
    early_b += [
        copies.start(state, padded.at[pl.ds(1, cx), pl.ds(1, cy)]),
        copies.start(source, load),
        copies.start(inverse, scale),
    ]
    if not last:
        picking = copies.start(take, picks)
    for copy in early:
        copy.wait()
    narrow = back[...].reshape(-1, lanes)
    coupled[...] = matmul(wide[...], narrow, ((1,), (0,)))
    for copy in early_b:
        copy.wait()
    padded[0, 1 : cy + 1] = rim[0].astype(F32)
    padded[cx + 1, 1 : cy + 1] = rim[1].astype(F32)
    for i in range(cx):
        padded[i + 1, 0] = rim[2, i].astype(F32)
        padded[i + 1, cy + 1] = rim[3, i].astype(F32)
    depth = lax.broadcasted_iota(jnp.int32, (cz, lanes), 0)

    def plane(m, carry):
        i, j = m // cy, m % cy
        here = padded[i + 1, j + 1]
        beside = padded[i + 2, j + 1] + padded[i, j + 1]
        beside = beside + padded[i + 1, j + 2] + padded[i + 1, j]
        beside = beside + jnp.where(depth == cz - 1, 0.0, pltpu.roll(here, cz - 1, 0))
        beside = beside + jnp.where(depth == 0, 0.0, pltpu.roll(here, 1, 0))
        first = pl.multiple_of(m * cz, cz)
        value = load[i, j] + beside - coupled[pl.ds(first, cz), :]
        fresh[i, j] = value * scale[i, j]
        return carry

    lax.fori_loop(0, cx * cy, plane, 0, unroll=4)
    done = [copies.start(fresh, out)]
    if not last:
        picking.wait()
        done += write_edges(fresh, picks, values, edges, chosen, rims, parity, copies)
    for copy in done:
        copy.wait()


def fem_call(parity, state, source, inverse, spread, returned, halos, take, last):
    cx, cy, cz, lanes = state.shape
    outs = [jax.ShapeDtypeStruct(state.shape, F32)]
    ins = [state, source, inverse, spread, returned, *halos]
    scratch = [
        ((cx + 2, cy + 2, cz, lanes), F32),
        (state.shape, F32),
        (state.shape, F32),
        (spread.shape, BF16),
        ((returned.shape[0], CAP, lanes), BF16),
        ((4, cx, cz, lanes), BF16),
        ((cx * cy * cz, lanes), F32),
        (state.shape, F32),
    ]
    if not last:
        ins.append(take)
        outs.append(jax.ShapeDtypeStruct((take.shape[0], lanes), BF16))
        outs += edge_shapes(state)
        scratch += [
            (take.shape, BF16),
            ((take.shape[0], lanes), BF16),
            ((4, cx, cz, lanes), BF16),
        ]
    return kernel_call(
        functools.partial(fem_body, last),
        ins,
        outs,
        scratch,
        16,
        4 * spread.size * lanes,
        "fem_last" if last else "fem_step",
        smem=[parity],
    )


def update_body(last, *refs):
    summed, density, source, diagonal = refs[:4]
    copies = None
    if last:
        out = refs[4]
        terms, here, load, scale, fresh, sems = refs[5:]
    else:
        right, out, spread, moment = refs[4:8]
        terms, here, load, scale, fresh, factor, narrow, short, sems = refs[8:]
    copies = Copies(sems)
    ins = [
        copies.start(summed, terms),
        copies.start(density, here),
        copies.start(source, load),
        copies.start(diagonal, scale),
    ]
    if not last:
        ins.append(copies.start(right, factor))
    for copy in ins:
        copy.wait()
    applied = jnp.sum(terms[...].astype(F32), axis=0)
    value = here[...] + (load[...] - applied) / scale[...]
    fresh[...] = value
    done = [copies.start(fresh, out)]
    if not last:
        rounded = value.astype(BF16)
        for k in range(narrow.shape[0]):
            narrow[k] = rounded
        done.append(copies.start(narrow, spread))
        short[...] = moments(rounded, factor).astype(BF16)
        done.append(copies.start(short, moment))
    for copy in done:
        copy.wait()


def update_call(summed, density, source, diagonal, right, last):
    outs = [jax.ShapeDtypeStruct(density.shape, F32)]
    ins = [summed, density, source, diagonal]
    scratch = [
        (summed.shape, BF16),
        (density.shape, F32),
        (density.shape, F32),
        (diagonal.shape, F32),
        (density.shape, F32),
    ]
    if not last:
        ins.append(right)
        outs += [
            jax.ShapeDtypeStruct(summed.shape, BF16),
            jax.ShapeDtypeStruct((density.shape[0], 128), BF16),
        ]
        scratch += [
            (right.shape, BF16),
            (summed.shape, BF16),
            ((density.shape[0], 128), BF16),
        ]
    return kernel_call(
        functools.partial(update_body, last),
        ins,
        outs,
        scratch,
        8,
        1 << 20,
        "update_last" if last else "update",
    )


def pick_body(joined, *refs):
    if joined:
        full, hot, values, moment, out = refs[:5]
        whole, mask, chosen, short, packed, sems = refs[5:]
    else:
        full, hot, out = refs[:3]
        whole, mask, packed, sems = refs[3:]
    copies = Copies(sems)
    ins = [copies.start(full, whole), copies.start(hot, mask)]
    if joined:
        ins += [copies.start(values, chosen), copies.start(moment, short)]
    for copy in ins:
        copy.wait()
    banks, lanes = packed.shape[0], packed.shape[2]
    picked = matmul(mask[...], whole[...], ((1,), (1,))).astype(BF16)
    picked = picked.reshape(banks, CAP, lanes)
    if joined:
        packed[:, :CAP] = chosen[...].reshape(banks, CAP, lanes)
        packed[:, CAP : 2 * CAP] = picked
        for bank in range(banks):
            packed[bank, 2 * CAP :] = short[...]
    else:
        packed[...] = picked
    copies.start(packed, out).wait()


def pick_call(full, hot, values, moment, banks):
    joined = values is not None
    rows = 2 * CAP + moment.shape[0] if joined else CAP
    lanes = full.shape[0]
    ins = [full, hot] + ([values, moment] if joined else [])
    scratch = [(x.shape, BF16) for x in ins] + [((banks, rows, lanes), BF16)]
    (out,) = kernel_call(
        functools.partial(pick_body, joined),
        ins,
        [jax.ShapeDtypeStruct((banks, rows, lanes), BF16)],
        scratch,
        5,
        2 * hot.size * lanes,
        "pick" if joined else "pick_first",
    )
    return out


def exchange(x, axis):
    return lax.all_to_all(x, axis, split_axis=0, concat_axis=0, tiled=True)


def swaps(x_first, x_second, axis):
    size = lax.axis_size(axis)
    inner = [(i, i ^ 1) for i in range(size)]
    outer = [(i, i + 1) if i % 2 else (i, i - 1) for i in range(1, size - 1)]
    return lax.ppermute(x_first, axis, inner), lax.ppermute(x_second, axis, outer)


def ordered(x, *others):
    return lax.optimization_barrier((x, others))[0]


def around(x, axis, shift):
    size = lax.axis_size(axis)
    return lax.ppermute(x, axis, [(i, (i + shift) % size) for i in range(size)])


def partner(x, axis):
    return lax.ppermute(x, axis, [(i, i ^ 1) for i in range(lax.axis_size(axis))])


def shards(
    fem_field,
    fem_source,
    reaction,
    bem_density,
    bem_source,
    bem_diagonal,
    near_blocks,
    near_pairs,
    low_left,
    low_right,
    centers,
    trace_cell,
    trace_bank,
    trace_row,
):
    fem_count = lax.axis_size("fem")
    bem_count = lax.axis_size("bem")
    fem_rank = lax.axis_index("fem")
    bem_rank = lax.axis_index("bem")
    excitations, local_rows = bem_density.shape
    share = excitations // fem_count
    per_dev, group, panel_rows, _ = near_blocks.shape
    panel_total, rank, _ = low_right.shape
    cells = reaction.size
    slots = trace_cell.shape[0]
    places = bem_count * CAP
    first_col = fem_rank * share
    own_first = bem_rank * per_dev

    parity = jnp.stack([fem_rank % 2, bem_rank % 2]).astype(jnp.int32)
    starts = jnp.stack([first_col, own_first]).astype(jnp.int32)
    sent, take, codes, *edges = setup_call(
        parity,
        starts,
        trace_bank.reshape(1, -1),
        trace_cell.reshape(1, -1),
        trace_row.reshape(1, -1),
        fem_field,
        bem_density,
        low_right,
        bem_count,
        share,
        per_dev,
    )
    cell_ids = jnp.arange(1, cells + 1, dtype=jnp.int32)
    spread = (cell_ids[:, None] == codes).astype(BF16)

    own_centers = lax.dynamic_slice_in_dim(centers, own_first, per_dev, 0)
    offsets = own_centers[:, None, :] - centers[None, :, :]
    kernel_rows = 1.0 / (1.0 + jnp.sum(offsets * offsets, axis=-1))
    panel_ids = jnp.arange(panel_total, dtype=jnp.int32)
    own_ids = own_first + jnp.arange(per_dev, dtype=jnp.int32)
    listed = jnp.any(near_pairs[:, :, None] == panel_ids[None, None, :], axis=1)
    listed = listed | (own_ids[:, None] == panel_ids[None, :])
    kernel_rows = jnp.where(listed, 0.0, kernel_rows)
    weights = jnp.repeat(kernel_rows.reshape(per_dev, bem_count, per_dev), rank, axis=2)
    weights = jnp.pad(weights.transpose(1, 0, 2), ((0, 0), (0, 0), (0, 128 - per_dev * rank)))
    factors = jnp.concatenate([low_left] * per_dev, axis=1)
    factors = jnp.pad(factors, ((0, 0), (0, 128 - per_dev * rank), (0, 0)))
    own_right = lax.dynamic_slice_in_dim(low_right, own_first, per_dev, 0)

    sources = lax.dynamic_slice_in_dim(near_pairs, fem_rank * group, group, 1)
    source_bank = sources // per_dev
    chip = jnp.mod(source_bank // 2 - bem_rank // 2 + 1, bem_count // 2)
    other = (source_bank + bem_rank) % 2
    table = ((chip * 2 + other) * per_dev + sources % per_dev).reshape(-1)
    table = jnp.concatenate([table, first_col[None]]).astype(jnp.int32)

    inverse = jnp.broadcast_to((1.0 / (6.0 + reaction))[..., None], fem_field.shape)
    density = lax.dynamic_slice_in_dim(bem_density, first_col, share, 0)
    source_part = lax.dynamic_slice_in_dim(bem_source, first_col, share, 0)
    diag_row = bem_diagonal[None, :]

    full = bem_density.astype(BF16)
    fem_state = fem_field
    received = exchange(sent, "bem")
    coded = received[:, CAP, 2 * CAP :].astype(F32)
    rows = (coded[:, :CAP] * 32.0 + coded[:, CAP:]).astype(jnp.int32).reshape(-1)
    hot = (rows[:, None] == jnp.arange(1, local_rows + 1, dtype=jnp.int32)).astype(BF16)
    for sweep in range(ITERS):
        last = sweep == ITERS - 1
        if sweep > 0:
            full = exchange(copies, "fem").reshape(excitations, local_rows)
            full = ordered(full, values)
        left = around(full, "bem", 2)
        right = around(full, "bem", -2)
        own = partner(full, "bem")
        parts = [left, partner(left, "bem"), full, own, right, partner(right, "bem")]
        if sweep > 0:
            sent = pick_call(full, hot, values, moment, bem_count)
            received = exchange(sent, "bem")
            returned = received
        if sweep == 0:
            halos = swaps(*edges[:2], "fem") + swaps(*edges[2:], "bem")
            table = ordered(table, halos, spread, inverse)
        partial = near_call(table, parts, near_blocks, received, hot, weights, factors)
        summed = exchange(partial.reshape(fem_count, share, local_rows), "fem")
        if sweep == 0:
            picked = pick_call(full, ordered(hot, partial), None, None, bem_count)
            returned = exchange(picked, "bem")
            summed = ordered(summed, picked)
        else:
            edges = ordered(tuple(edges), partial)
            halos = swaps(*edges[:2], "fem") + swaps(*edges[2:], "bem")
            summed = ordered(summed, halos)
        if last:
            density = update_call(summed, density, source_part, diag_row, own_right, last)[0]
            state = fem_state
        else:
            density, copies, moment = update_call(
                summed, density, source_part, diag_row, own_right, last
            )
            state = ordered(fem_state, copies)
        fem_state, *rest = fem_call(
            parity, state, fem_source, inverse, spread, returned, halos, take, last
        )
        if not last:
            values, *edges = rest
    return (fem_state, density)


def solution(mesh):
    return jax.shard_map(
        shards,
        mesh=mesh,
        in_specs=(
            P("fem", "bem", None, None),
            P("fem", "bem", None, None),
            P("fem", "bem", None),
            P(None, "bem"),
            P(None, "bem"),
            P("bem"),
            P("bem", "fem", None, None),
            P("bem", None),
            P("bem", None, None),
            P(),
            P(),
            P(("fem", "bem")),
            P(("fem", "bem"), None),
            P(("fem", "bem")),
        ),
        out_specs=(P("fem", "bem", None, None), P("fem", "bem")),
        check_vma=False,
    )
```

```python
import functools

import jax
import jax.numpy as jnp
from jax import lax
from jax.experimental import pallas as pl
from jax.experimental.pallas import tpu as pltpu
from jax.sharding import PartitionSpec as P

CAP = 32
ITERS = 3
COVER = 20_000_000_000
HIGHEST = lax.Precision.HIGHEST
BF16 = jnp.bfloat16
F32 = jnp.float32


def matmul(left, right, dims):
    return lax.dot_general(left, right, (dims, ((), ())), preferred_element_type=F32)


def kernel_call(body, args, outs, scratch, copies, flops, name, smem=()):
    hbm = pl.BlockSpec(memory_space=pltpu.HBM)
    scalar = pl.BlockSpec(memory_space=pltpu.SMEM)
    args = [*smem, *args]
    return pl.pallas_call(
        body,
        out_shape=outs,
        in_specs=[scalar] * len(smem) + [hbm] * (len(args) - len(smem)),
        out_specs=[hbm] * len(outs),
        scratch_shapes=[pltpu.VMEM(s, t) for s, t in scratch] + [pltpu.SemaphoreType.DMA((copies,))],
        compiler_params=pltpu.CompilerParams(vmem_limit_bytes=64 << 20),
        cost_estimate=pl.CostEstimate(
            flops=flops,
            bytes_accessed=sum(x.size * x.dtype.itemsize for x in args),
            transcendentals=0,
        ),
        name=name,
    )(*args)


class Copies:
    def __init__(self, sems):
        self.sems, self.count = sems, 0

    def start(self, source, target):
        copy = pltpu.make_async_copy(source, target, self.sems.at[self.count])
        self.count += 1
        copy.start()
        return copy


def whereabouts():
    bem = lax.axis_index("bem")
    core, odd = bem % 2, bem // 2 % 2
    inside = (bem > 0) & (bem < lax.axis_size("bem") - 1)
    return (lax.axis_index("fem") % 2, core, odd, (core + odd + 1) % 2, inside)


def near_body(pairs, *refs):
    parts = refs[:6]
    blocks, received, hot, weights, factors, out = refs[6:12]
    panels, held, got, mask, mix, factor, total, narrow, sems = refs[12:]
    per_dev, group, rows, _ = blocks.shape
    share = panels.shape[1] // lax.axis_size("fem")
    rank = factors.shape[1]
    copies = Copies(sems)
    small = [
        copies.start(received, got),
        copies.start(hot, mask),
        copies.start(weights, mix),
    ]
    for k in range(per_dev):
        small.append(copies.start(factors, factor.at[:, k * rank : (k + 1) * rank]))
    moved = []
    for place, ref in enumerate(parts):
        for half in range(per_dev):
            moved.append(
                copies.start(
                    ref.at[pl.ds(0, panels.shape[1]), half * rows : (half + 1) * rows],
                    panels.at[place * per_dev + half],
                )
            )
    loads = []
    for half in range(per_dev):
        for step in range(group):
            loads.append(copies.start(blocks.at[half, step], held.at[half * group + step]))
    factor[:, per_dev * rank :] = jnp.zeros_like(factor[:, per_dev * rank :])
    for copy in small:
        copy.wait()
    fem, bem, banks = lax.axis_index("fem"), lax.axis_index("bem"), lax.axis_size("bem")
    values = got[:, :CAP, :].reshape(-1, got.shape[2])
    traced = matmul(values, mask[...], ((0,), (0,)))
    start = pl.multiple_of(fem * share, share)
    for half in range(per_dev):
        mixed = jnp.zeros((share, got.shape[2]), F32)
        for bank in range(got.shape[0]):
            mixed = mixed + mix[bank, half : half + 1, :] * got[
                bank, got.shape[1] - share :, :
            ].astype(F32)
        upper = mixed.astype(BF16)
        lower = (mixed - upper.astype(F32)).astype(BF16)
        far = matmul(upper, factor[half], ((1,), (0,))) + matmul(lower, factor[half], ((1,), (0,)))
        total[half] = traced[:, half * rows : (half + 1) * rows]
        total[half, pl.ds(start, share), :] += far
    for copy in moved:
        copy.wait()
    done = []
    for half in range(per_dev):
        summed = total[half]
        for step in range(group):
            source = pairs[half, fem * group + step]
            bank = source // per_dev
            chip = (bank // 2 - bem // 2 + 1 + banks // 2) % (banks // 2)
            chip = jnp.where(bem // 2 % 2 == 1, chip, 2 - chip)
            place = (chip * 2 + (bank + bem) % 2) * per_dev + source % per_dev
            loads[half * group + step].wait()
            summed = summed + matmul(panels[place], held[half * group + step], ((1,), (0,)))
        narrow[half] = summed.astype(BF16)
        done.append(copies.start(narrow.at[half], out.at[:, half * rows : (half + 1) * rows]))
    for copy in done:
        copy.wait()


def near_call(pairs, parts, near_blocks, received, hot, weights, factors):
    per_dev, group, rows, _ = near_blocks.shape
    excitations = parts[2].shape[0]
    return kernel_call(
        near_body,
        [*parts, near_blocks, received, hot, weights, factors],
        [jax.ShapeDtypeStruct((excitations, per_dev * rows), BF16)],
        [
            ((6 * per_dev, excitations, rows), BF16),
            ((per_dev * group, rows, rows), BF16),
            (received.shape, BF16),
            (hot.shape, BF16),
            (weights.shape, F32),
            ((per_dev, weights.shape[2], rows), BF16),
            ((per_dev, excitations, rows), F32),
            ((per_dev, excitations, rows), BF16),
        ],
        3 + per_dev + 6 * per_dev + per_dev * group + per_dev,
        2 * excitations * near_blocks.size // rows * rows,
        "near",
        smem=[pairs],
    )[0]


def gate_call(kept, *arrived):
    hbm = pl.BlockSpec(memory_space=pltpu.HBM)
    return pl.pallas_call(
        lambda *refs: None,
        out_shape=jax.ShapeDtypeStruct(kept.shape, kept.dtype),
        in_specs=[hbm] * (1 + len(arrived)),
        out_specs=hbm,
        input_output_aliases={0: 0},
        compiler_params=pltpu.CompilerParams(vmem_limit_bytes=64 << 20),
        cost_estimate=pl.CostEstimate(flops=COVER, bytes_accessed=0, transcendentals=0),
        name="gate",
    )(kept, *arrived)


def write_edges(state, take, outs, chosen, rims, sides, marks, copies):
    values, first, second, rows, near = outs
    cx, cy, cz, lanes = state.shape
    rims[0] = state[0].astype(BF16)
    rims[1] = state[cx - 1].astype(BF16)
    for i in range(cx):
        sides[0, :, i * lanes : (i + 1) * lanes] = state[i, 0].astype(BF16)
        sides[1, :, i * lanes : (i + 1) * lanes] = state[i, cy - 1].astype(BF16)
    done = [
        copies.start(rims.at[1 - marks[0]], first),
        copies.start(rims.at[marks[0]], second),
        copies.start(sides, rows),
        copies.start(sides.at[1 - marks[1]], near),
    ]
    narrow = state[...].reshape(cx * cy * cz, lanes).astype(BF16)
    chosen[...] = matmul(take[...], narrow, ((1,), (0,))).astype(BF16)
    done.append(copies.start(chosen, values))
    return done


def edge_shapes(state, places):
    cx, cy, cz, lanes = state.shape
    return [
        jax.ShapeDtypeStruct((places, lanes), BF16),
        jax.ShapeDtypeStruct((cy, cz, lanes), BF16),
        jax.ShapeDtypeStruct((cy, cz, lanes), BF16),
        jax.ShapeDtypeStruct((2, cz, cx * lanes), BF16),
        jax.ShapeDtypeStruct((cz, cx * lanes), BF16),
    ]


def edge_scratch(state, places):
    cx, cy, cz, lanes = state.shape
    return [
        ((places, lanes), BF16),
        ((2, cy, cz, lanes), BF16),
        ((2, cz, cx * lanes), BF16),
    ]


def slot_places(bank_r):
    slots = bank_r.shape[1]
    down = lax.broadcasted_iota(jnp.int32, (slots, slots), 0)
    over = lax.broadcasted_iota(jnp.int32, (slots, slots), 1)

    def column(x):
        return jnp.sum(jnp.where(down == over, x, 0), axis=1, keepdims=True)

    bank_c = column(bank_r)
    same = bank_c == bank_r
    place_r = bank_r * CAP + jnp.sum(
        jnp.where(same & (down < over), 1, 0), axis=0, keepdims=True
    )
    return place_r, column(place_r), column


def index_body(bank, row, sent, banks_v, rows_v, packed, sems):
    copies = Copies(sems)
    for copy in [copies.start(bank, banks_v), copies.start(row, rows_v)]:
        copy.wait()
    banks, cap, lanes = packed.shape
    place_r, _, _ = slot_places(banks_v[...])
    hit = lax.broadcasted_iota(jnp.int32, (banks * cap, bank.shape[1]), 0) == place_r
    code = jnp.sum(jnp.where(hit, rows_v[...] + 1, 0), axis=1, keepdims=True)
    lane = lax.broadcasted_iota(jnp.int32, (banks * cap, lanes), 1)
    digits = jnp.where(lane == 0, code // 32, jnp.where(lane == 1, code % 32, 0))
    packed[...] = digits.astype(F32).astype(BF16).reshape(banks, cap, lanes)
    copies.start(packed, sent).wait()


def index_call(bank, row, banks, lanes):
    packed = (banks, CAP, lanes)
    return kernel_call(
        index_body,
        [bank, row],
        [jax.ShapeDtypeStruct(packed, BF16)],
        [(bank.shape, jnp.int32), (row.shape, jnp.int32), (packed, BF16)],
        3,
        1 << 20,
        "index",
    )[0]


def first_panel(part):
    return lax.axis_index("bem") * part.shape[0]


def setup_body(*refs):
    marks = whereabouts()
    bank, cell, state, density, right = refs[:5]
    take, codes, moment = refs[5:8]
    outs = refs[8:13]
    banks_v, cells_v, here, share_v, factor, picks, coded, short, chosen, rims, sides, sems = refs[13:]
    copies = Copies(sems)
    small = [copies.start(bank, banks_v), copies.start(cell, cells_v)]
    share = share_v.shape[0]
    start = pl.multiple_of(lax.axis_index("fem") * share, share)
    large = [
        copies.start(density.at[pl.ds(start, share)], share_v),
        copies.start(right.at[pl.ds(first_panel(factor), factor.shape[0])], factor),
        copies.start(state, here),
    ]
    for copy in small:
        copy.wait()
    slots = bank.shape[1]
    places, cells = take.shape
    cell_r = cells_v[...] + 1
    place_r, place_c, column = slot_places(banks_v[...])
    hit = lax.broadcasted_iota(jnp.int32, (places, slots), 0) == place_r
    cell_c = jnp.sum(jnp.where(hit, cell_r, 0), axis=1, keepdims=True)
    ids = lax.broadcasted_iota(jnp.int32, (places, cells), 1) + 1
    picks[...] = (cell_c == ids).astype(F32).astype(BF16)
    out = [copies.start(picks, take)]
    hit = lax.broadcasted_iota(jnp.int32, (slots, places), 1) == place_c
    coded[...] = jnp.sum(jnp.where(hit, column(cell_r), 0), axis=0, keepdims=True)
    out.append(copies.start(coded, codes))
    for copy in large:
        copy.wait()
    out += write_edges(here, picks, outs, chosen, rims, sides, marks, copies)
    short[...] = moments(share_v[...].astype(BF16), factor).astype(BF16)
    out.append(copies.start(short, moment))
    for copy in out:
        copy.wait()


def setup_call(bank, cell, state, density, right, banks, share, per_dev):
    cx, cy, cz, lanes = state.shape
    slots = bank.shape[1]
    places = banks * CAP
    take = jax.ShapeDtypeStruct((places, cx * cy * cz), BF16)
    return kernel_call(
        setup_body,
        [bank, cell, state, density, right],
        [
            take,
            jax.ShapeDtypeStruct((1, places), jnp.int32),
            jax.ShapeDtypeStruct((share, 128), BF16),
        ]
        + edge_shapes(state, places),
        [
            ((1, slots), jnp.int32),
            ((1, slots), jnp.int32),
            (state.shape, F32),
            ((share, density.shape[1]), F32),
            ((per_dev, *right.shape[1:]), BF16),
            (take.shape, BF16),
            ((1, places), jnp.int32),
            ((share, 128), BF16),
        ]
        + edge_scratch(state, places),
        13,
        2 * take.size * lanes,
        "setup",
    )


def moments(rounded, factor):
    per_dev, rank, rows = factor.shape
    sums = [
        matmul(rounded[:, q * rows : (q + 1) * rows], factor[q], ((1,), (1,)))
        for q in range(per_dev)
    ]
    sums.append(jnp.zeros((rounded.shape[0], 128 - per_dev * rank), F32))
    return jnp.concatenate(sums, axis=1)


def tables_body(
    codes, centers, pairs, reaction, spread, weights, inverse,
    codes_v, places, listed_v, scale, wide, mix, full, sems,
):
    copies = Copies(sems)
    ins = [
        copies.start(codes, codes_v),
        copies.start(centers, places),
        copies.start(pairs, listed_v),
        copies.start(reaction, scale),
    ]
    for copy in ins:
        copy.wait()
    cx, cy, cz, lanes = full.shape
    scale[...] = 1.0 / (6.0 + scale[...])
    down = lax.broadcasted_iota(jnp.int32, (cz, cz), 0)
    over = lax.broadcasted_iota(jnp.int32, (cz, cz), 1)

    def plane(m, carry):
        i, j = m // cy, m % cy
        along_lanes = scale[i, pl.ds(j, 1), :]
        factor = jnp.sum(jnp.where(down == over, along_lanes, 0.0), axis=1, keepdims=True)
        full[i, j] = jnp.broadcast_to(factor, (cz, lanes))
        return carry

    lax.fori_loop(0, cx * cy, plane, 0, unroll=8)
    wanted = codes_v[...]
    rows = 256
    done = []
    for k in range(wide.shape[0] // rows):
        ids = lax.broadcasted_iota(jnp.int32, (rows, wanted.shape[1]), 0) + (k * rows + 1)
        wide[k * rows : (k + 1) * rows] = (ids == wanted).astype(F32).astype(BF16)
    done += [copies.start(wide, spread), copies.start(full, inverse)]
    banks, per_dev, lanes = mix.shape
    panels = places.shape[1]
    rank = lanes // 2 // per_dev
    near = listed_v[...]
    ids = lax.broadcasted_iota(jnp.int32, (panels, near.shape[1]), 0)
    own = lax.broadcasted_iota(jnp.int32, (panels, 1), 0)
    panel = lax.broadcasted_iota(jnp.int32, (panels, lanes), 0)
    lane = lax.broadcasted_iota(jnp.int32, (panels, lanes), 1)
    spots = places[...]
    square = [lax.broadcasted_iota(jnp.int32, (panels, panels), d) for d in (0, 1)]
    which = lax.broadcasted_iota(jnp.int32, spots.shape, 1)
    own_first = lax.axis_index("bem") * per_dev
    for p in range(per_dev):
        here = jnp.sum(jnp.where(which == own_first + p, spots, 0.0), axis=1, keepdims=True)
        offset = here - spots
        apart = jnp.sum(offset * offset, axis=0, keepdims=True)
        apart = jnp.where(square[0] == square[1], apart, 0.0)
        kernel = 1.0 / (1.0 + jnp.sum(apart, axis=1, keepdims=True))
        hits = jnp.sum(jnp.where(ids == near[p : p + 1], 1, 0), axis=1, keepdims=True)
        kernel = jnp.where((hits > 0) | (own == own_first + p), 0.0, kernel)
        for k in range(banks):
            there = (panel == per_dev * k + lane // rank) & (lane < per_dev * rank)
            mix[k, p : p + 1] = jnp.sum(jnp.where(there, kernel, 0.0), axis=0, keepdims=True)
    done.append(copies.start(mix, weights))
    for copy in done:
        copy.wait()


def tables_call(codes, centers, pairs, reaction, lanes, banks):
    cells = reaction.size
    inverse = jax.ShapeDtypeStruct((*reaction.shape, lanes), F32)
    spread = jax.ShapeDtypeStruct((cells, codes.shape[1]), BF16)
    weights = jax.ShapeDtypeStruct((banks, pairs.shape[0], 128), F32)
    return kernel_call(
        tables_body,
        [codes, centers, pairs, reaction],
        [spread, weights, inverse],
        [
            (codes.shape, jnp.int32),
            (centers.shape, F32),
            (pairs.shape, jnp.int32),
            (reaction.shape, F32),
            (spread.shape, BF16),
            (weights.shape, F32),
            (inverse.shape, F32),
        ],
        7,
        1 << 20,
        "tables",
    )


def fem_body(last, *refs):
    marks = whereabouts()
    state, source, inverse, spread, returned = refs[:5]
    first, second, near, inner, outer = refs[5:10]
    if last:
        out = refs[10]
        padded, load, scale, wide, back, rim, side, coupled, fresh, sems = refs[11:]
    else:
        take, out = refs[10:12]
        outs = refs[12:17]
        padded, load, scale, wide, back, rim, side, coupled, fresh = refs[17:26]
        picks, chosen, rims, sides, sems = refs[26:]
    cx, cy, cz, lanes = state.shape
    rows = inner.shape[0] - cz
    copies = Copies(sems)
    early = [copies.start(spread, wide), copies.start(returned.at[:, pl.ds(CAP, CAP)], back)]
    late = [
        copies.start(first, rim.at[1 - marks[0]]),
        copies.start(second, rim.at[marks[0]]),
        copies.start(near, side.at[2]),
        copies.start(inner.at[pl.ds(rows, cz)], side.at[0]),
        copies.start(outer.at[pl.ds(rows, cz)], side.at[1]),
        copies.start(state, padded.at[pl.ds(1, cx), pl.ds(1, cy)]),
        copies.start(source, load),
        copies.start(inverse, scale),
    ]
    if not last:
        picking = copies.start(take, picks)
    for copy in early:
        copy.wait()
    coupled[...] = matmul(wide[...], back[...].reshape(-1, lanes), ((1,), (0,)))
    for copy in late:
        copy.wait()
    padded[0, 1 : cy + 1] = rim[0].astype(F32)
    padded[cx + 1, 1 : cy + 1] = rim[1].astype(F32)
    far, close = marks[1] * (cy + 1), (1 - marks[1]) * (cy + 1)
    held = jnp.full((cz, lanes), marks[4].astype(jnp.int32), jnp.int32) > 0
    for i in range(cx):
        part = side[marks[3], :, i * lanes : (i + 1) * lanes].astype(F32)
        padded[i + 1, far] = jnp.where(held, part, 0.0)
        padded[i + 1, close] = side[2, :, i * lanes : (i + 1) * lanes].astype(F32)
    depth = lax.broadcasted_iota(jnp.int32, (cz, lanes), 0)

    def plane(m, carry):
        i, j = m // cy, m % cy
        here = padded[i + 1, j + 1]
        beside = padded[i + 2, j + 1] + padded[i, j + 1]
        beside = beside + padded[i + 1, j + 2] + padded[i + 1, j]
        beside = beside + jnp.where(depth == cz - 1, 0.0, pltpu.roll(here, cz - 1, 0))
        beside = beside + jnp.where(depth == 0, 0.0, pltpu.roll(here, 1, 0))
        start = pl.multiple_of(m * cz, cz)
        value = load[i, j] + beside - coupled[pl.ds(start, cz), :]
        fresh[i, j] = value * scale[i, j]
        return carry

    lax.fori_loop(0, cx * cy, plane, 0, unroll=4)
    done = [copies.start(fresh, out)]
    if not last:
        picking.wait()
        done += write_edges(fresh, picks, outs, chosen, rims, sides, marks, copies)
    for copy in done:
        copy.wait()


def fem_call(state, source, inverse, spread, returned, halos, take, last):
    cx, cy, cz, lanes = state.shape
    outs = [jax.ShapeDtypeStruct(state.shape, F32)]
    ins = [state, source, inverse, spread, returned, *halos]
    scratch = [
        ((cx + 2, cy + 2, cz, lanes), F32),
        (state.shape, F32),
        (state.shape, F32),
        (spread.shape, BF16),
        ((returned.shape[0], CAP, lanes), BF16),
        ((2, cy, cz, lanes), BF16),
        ((3, cz, cx * lanes), BF16),
        ((cx * cy * cz, lanes), F32),
        (state.shape, F32),
    ]
    if not last:
        ins.append(take)
        outs += edge_shapes(state, take.shape[0])
        scratch += [(take.shape, BF16)] + edge_scratch(state, take.shape[0])
    return kernel_call(
        functools.partial(fem_body, last),
        ins,
        outs,
        scratch,
        17,
        4 * spread.size * lanes,
        "fem_last" if last else "fem_step",
    )


def share_of(whole, part, start):
    return whole if whole.shape == part.shape else whole.at[pl.ds(start, part.shape[0])]


def update_body(last, *refs):
    summed, density, source, diagonal = refs[:4]
    copies = None
    if last:
        out = refs[4]
        terms, here, load, scale, fresh, sems = refs[5:]
    else:
        right, out, spread, moment = refs[4:8]
        terms, here, load, scale, fresh, factor, narrow, short, sems = refs[8:]
    copies = Copies(sems)
    ins = [
        copies.start(summed, terms),
        copies.start(share_of(density, here, pl.multiple_of(lax.axis_index("fem") * here.shape[0], here.shape[0])), here),
        copies.start(share_of(source, load, pl.multiple_of(lax.axis_index("fem") * load.shape[0], load.shape[0])), load),
        copies.start(diagonal, scale),
    ]
    if not last:
        ins.append(copies.start(share_of(right, factor, first_panel(factor)), factor))
    for copy in ins:
        copy.wait()
    applied = jnp.sum(terms[...].astype(F32), axis=0)
    value = here[...] + (load[...] - applied) / scale[...]
    fresh[...] = value
    done = [copies.start(fresh, out)]
    if not last:
        rounded = value.astype(BF16)
        for k in range(narrow.shape[0]):
            narrow[k] = rounded
        done.append(copies.start(narrow, spread))
        short[...] = moments(rounded, factor).astype(BF16)
        done.append(copies.start(short, moment))
    for copy in done:
        copy.wait()


def update_call(summed, density, source, diagonal, right, per_dev, last):
    shape = summed.shape[1:]
    outs = [jax.ShapeDtypeStruct(shape, F32)]
    ins = [summed, density, source, diagonal]
    scratch = [
        (summed.shape, BF16),
        (shape, F32),
        (shape, F32),
        (diagonal.shape, F32),
        (shape, F32),
    ]
    if not last:
        ins.append(right)
        outs += [
            jax.ShapeDtypeStruct(summed.shape, BF16),
            jax.ShapeDtypeStruct((shape[0], 128), BF16),
        ]
        scratch += [
            ((per_dev, *right.shape[1:]), BF16),
            (summed.shape, BF16),
            ((shape[0], 128), BF16),
        ]
    return kernel_call(
        functools.partial(update_body, last),
        ins,
        outs,
        scratch,
        8,
        1 << 20,
        "update_last" if last else "update",
    )


def pick_body(first, *refs):
    marks = whereabouts()
    full, hot, values, moment, rows, sent, inner, outer = refs[:8]
    if first:
        out, whole, mask, chosen, short, sides, packed, coded, sems = refs[8:]
    else:
        whole, mask, chosen, short, sides, packed, sems = refs[8:]
    copies = Copies(sems)
    get = copies.start(hot, coded if first else mask)
    ins = [
        copies.start(full, whole),
        copies.start(rows, sides),
        copies.start(values, chosen),
        copies.start(moment, short),
    ]
    get.wait()
    done = []
    if first:
        digits = coded[...].reshape(mask.shape[0], -1).astype(F32)
        code = (digits[:, :1] * 32.0 + digits[:, 1:2]).astype(jnp.int32)
        ids = lax.broadcasted_iota(jnp.int32, mask.shape, 1) + 1
        mask[...] = (code == ids).astype(F32).astype(BF16)
        done.append(copies.start(mask, out))
    for copy in ins:
        copy.wait()
    height = whole.shape[0]
    cz = sides.shape[1]
    for target, which in ((inner, 1 - marks[2]), (outer, marks[2])):
        done.append(copies.start(whole, target.at[pl.ds(0, height)]))
        done.append(copies.start(sides.at[which], target.at[pl.ds(height, cz)]))
    banks, lanes = packed.shape[0], packed.shape[2]
    picked = matmul(mask[...], whole[...], ((1,), (1,))).astype(BF16)
    packed[:, :CAP] = chosen[...].reshape(banks, CAP, lanes)
    packed[:, CAP : 2 * CAP] = picked.reshape(banks, CAP, lanes)
    for bank in range(banks):
        packed[bank, 2 * CAP :] = short[...]
    done.append(copies.start(packed, sent))
    for copy in done:
        copy.wait()


def pick_call(full, hot, values, moment, rows, banks):
    first = hot.ndim == 3
    lanes, width = full.shape
    mask = jax.ShapeDtypeStruct((values.shape[0], width), BF16)
    sent = jax.ShapeDtypeStruct((banks, 2 * CAP + moment.shape[0], lanes), BF16)
    swap = jax.ShapeDtypeStruct((lanes + rows.shape[1], width), BF16)
    scratch = [(full.shape, BF16), (mask.shape, BF16), (values.shape, BF16)]
    scratch += [(moment.shape, BF16), (rows.shape, BF16), (sent.shape, BF16)]
    if first:
        scratch.append((hot.shape, BF16))
    return kernel_call(
        functools.partial(pick_body, first),
        [full, hot, values, moment, rows],
        [sent, swap, swap] + [mask] * first,
        scratch,
        11,
        2 * mask.size * lanes,
        "pick_first" if first else "pick",
    )


def exchange(x, axis):
    return lax.all_to_all(x, axis, split_axis=0, concat_axis=0, tiled=True)


def swaps(x_first, x_second, axis):
    size = lax.axis_size(axis)
    inner = [(i, i ^ 1) for i in range(size)]
    outer = [(i, i + 1) if i % 2 else (i, i - 1) for i in range(1, size - 1)]
    return lax.ppermute(x_first, axis, inner), lax.ppermute(x_second, axis, outer)


def chip_swaps(x_inner, x_outer, axis):
    size = lax.axis_size(axis)
    inner = [(i, i ^ 2) for i in range(size)]
    outer = [(i, (i + 2 if i // 2 % 2 else i - 2) % size) for i in range(size)]
    return lax.ppermute(x_inner, axis, inner), lax.ppermute(x_outer, axis, outer)


def ordered(x, *others):
    return lax.optimization_barrier((x, others))[0]


def partner(x, axis):
    return lax.ppermute(x, axis, [(i, i ^ 1) for i in range(lax.axis_size(axis))])


def shards(
    fem_field,
    fem_source,
    reaction,
    bem_density,
    bem_source,
    bem_diagonal,
    near_blocks,
    near_pairs,
    low_left,
    low_right,
    centers,
    trace_cell,
    trace_bank,
    trace_row,
):
    fem_count = lax.axis_size("fem")
    bem_count = lax.axis_size("bem")
    excitations, local_rows = bem_density.shape
    share = excitations // fem_count
    per_dev, group, panel_rows, _ = near_blocks.shape
    bank = trace_bank.reshape(1, -1)
    asked = exchange(index_call(bank, trace_row.reshape(1, -1), bem_count, excitations), "bem")
    take, codes, moment, values, *edges = setup_call(
        bank,
        trace_cell.reshape(1, -1),
        fem_field,
        bem_density,
        low_right,
        bem_count,
        share,
        per_dev,
    )
    spread, weights, inverse = tables_call(
        codes, centers.T, near_pairs, reaction, excitations, bem_count
    )

    diag_row = bem_diagonal[None, :]

    full = bem_density.astype(BF16)
    fem_state, density, hot = fem_field, bem_density, asked
    for sweep in range(ITERS):
        last = sweep == ITERS - 1
        if sweep > 0:
            full = exchange(copies, "fem").reshape(excitations, local_rows)
        first, second, rows, near = edges
        sent, inner, outer, *mask = pick_call(full, hot, values, moment, rows, bem_count)
        if mask:
            (hot,) = mask
        inner, outer = chip_swaps(inner, outer, "bem")
        received = exchange(sent, "bem")
        other_inner, other_outer = partner(inner, "bem"), partner(outer, "bem")
        parts = [inner, other_inner, full, partner(full, "bem"), outer, other_outer]
        first, second, near = ordered((first, second, near), sent)
        halos = swaps(first, second, "fem") + (partner(near, "bem"),)
        weights = gate_call(weights, received, *halos, *([spread] if sweep == 0 else []))
        partial = near_call(near_pairs, parts, near_blocks, received, hot, weights, low_left)
        summed = exchange(partial.reshape(fem_count, share, local_rows), "fem")
        fem_state, *rest = fem_call(
            ordered(fem_state, partial),
            fem_source,
            inverse,
            spread,
            received,
            (*halos, other_inner, other_outer),
            take,
            last,
        )
        density, *more = update_call(
            ordered(summed, fem_state),
            density,
            bem_source,
            diag_row,
            low_right,
            per_dev,
            last,
        )
        if not last:
            copies, moment = more
            values, *edges = rest
    return (fem_state, density)


def solution(mesh):
    return jax.shard_map(
        shards,
        mesh=mesh,
        in_specs=(
            P("fem", "bem", None, None),
            P("fem", "bem", None, None),
            P("fem", "bem", None),
            P(None, "bem"),
            P(None, "bem"),
            P("bem"),
            P("bem", "fem", None, None),
            P("bem", None),
            P("bem", None, None),
            P(),
            P(),
            P(("fem", "bem")),
            P(("fem", "bem"), None),
            P(("fem", "bem")),
        ),
        out_specs=(P("fem", "bem", None, None), P("fem", "bem")),
        check_vma=False,
    )
```

```python
import functools

import jax
import jax.numpy as jnp
from jax import lax
from jax.experimental import pallas as pl
from jax.experimental.pallas import tpu as pltpu
from jax.sharding import PartitionSpec as P

CAP = 32
ITERS = 3
COVER = 20_000_000_000
HIGHEST = lax.Precision.HIGHEST
BF16 = jnp.bfloat16
F32 = jnp.float32


def matmul(left, right, dims):
    return lax.dot_general(left, right, (dims, ((), ())), preferred_element_type=F32)


def kernel_call(body, args, outs, scratch, copies, flops, name, smem=()):
    hbm = pl.BlockSpec(memory_space=pltpu.HBM)
    scalar = pl.BlockSpec(memory_space=pltpu.SMEM)
    args = [*smem, *args]
    return pl.pallas_call(
        body,
        out_shape=outs,
        in_specs=[scalar] * len(smem) + [hbm] * (len(args) - len(smem)),
        out_specs=[hbm] * len(outs),
        scratch_shapes=[pltpu.VMEM(s, t) for s, t in scratch] + [pltpu.SemaphoreType.DMA((copies,))],
        compiler_params=pltpu.CompilerParams(vmem_limit_bytes=64 << 20),
        cost_estimate=pl.CostEstimate(
            flops=flops,
            bytes_accessed=sum(x.size * x.dtype.itemsize for x in args),
            transcendentals=0,
        ),
        name=name,
    )(*args)


class Copies:
    def __init__(self, sems):
        self.sems, self.count = sems, 0

    def start(self, source, target):
        copy = pltpu.make_async_copy(source, target, self.sems.at[self.count])
        self.count += 1
        copy.start()
        return copy


def whereabouts():
    bem = lax.axis_index("bem")
    core, odd = bem % 2, bem // 2 % 2
    inside = (bem > 0) & (bem < lax.axis_size("bem") - 1)
    return (lax.axis_index("fem") % 2, core, odd, (core + odd + 1) % 2, inside)


def near_body(pairs, *refs):
    parts = refs[:6]
    blocks, received, hot, weights, factors, out = refs[6:12]
    panels, held, got, mask, mix, factor, total, narrow, sems = refs[12:]
    per_dev, group, rows, _ = blocks.shape
    share = panels.shape[1] // lax.axis_size("fem")
    rank = factors.shape[1]
    copies = Copies(sems)
    small = [
        copies.start(received, got),
        copies.start(hot, mask),
        copies.start(weights, mix),
    ]
    for k in range(per_dev):
        small.append(copies.start(factors, factor.at[:, k * rank : (k + 1) * rank]))
    moved = []
    for place, ref in enumerate(parts):
        for half in range(per_dev):
            moved.append(
                copies.start(
                    ref.at[pl.ds(0, panels.shape[1]), half * rows : (half + 1) * rows],
                    panels.at[place * per_dev + half],
                )
            )
    loads = []
    for half in range(per_dev):
        for step in range(group):
            loads.append(copies.start(blocks.at[half, step], held.at[half * group + step]))
    factor[:, per_dev * rank :] = jnp.zeros_like(factor[:, per_dev * rank :])
    for copy in small:
        copy.wait()
    fem, bem, banks = lax.axis_index("fem"), lax.axis_index("bem"), lax.axis_size("bem")
    values = got[:, :CAP, :].reshape(-1, got.shape[2])
    traced = matmul(values, mask[...], ((0,), (0,)))
    start = pl.multiple_of(fem * share, share)
    for half in range(per_dev):
        mixed = jnp.zeros((share, got.shape[2]), F32)
        for bank in range(got.shape[0]):
            mixed = mixed + mix[bank, half : half + 1, :] * got[
                bank, got.shape[1] - share :, :
            ].astype(F32)
        upper = mixed.astype(BF16)
        lower = (mixed - upper.astype(F32)).astype(BF16)
        far = matmul(upper, factor[half], ((1,), (0,))) + matmul(lower, factor[half], ((1,), (0,)))
        total[half] = traced[:, half * rows : (half + 1) * rows]
        total[half, pl.ds(start, share), :] += far
    for copy in moved:
        copy.wait()
    done = []
    for half in range(per_dev):
        summed = total[half]
        for step in range(group):
            source = pairs[half, fem * group + step]
            bank = source // per_dev
            chip = (bank // 2 - bem // 2 + 1 + banks // 2) % (banks // 2)
            chip = jnp.where(bem // 2 % 2 == 1, chip, 2 - chip)
            place = (chip * 2 + (bank + bem) % 2) * per_dev + source % per_dev
            loads[half * group + step].wait()
            summed = summed + matmul(panels[place], held[half * group + step], ((1,), (0,)))
        narrow[half] = summed.astype(BF16)
        done.append(copies.start(narrow.at[half], out.at[:, half * rows : (half + 1) * rows]))
    for copy in done:
        copy.wait()


def near_call(pairs, parts, near_blocks, received, hot, weights, factors):
    per_dev, group, rows, _ = near_blocks.shape
    excitations = parts[2].shape[0]
    return kernel_call(
        near_body,
        [*parts, near_blocks, received, hot, weights, factors],
        [jax.ShapeDtypeStruct((excitations, per_dev * rows), BF16)],
        [
            ((6 * per_dev, excitations, rows), BF16),
            ((per_dev * group, rows, rows), BF16),
            (received.shape, BF16),
            (hot.shape, BF16),
            (weights.shape, F32),
            ((per_dev, weights.shape[2], rows), BF16),
            ((per_dev, excitations, rows), F32),
            ((per_dev, excitations, rows), BF16),
        ],
        3 + per_dev + 6 * per_dev + per_dev * group + per_dev,
        2 * excitations * near_blocks.size // rows * rows,
        "near",
        smem=[pairs],
    )[0]


def gate_call(kept, *arrived):
    hbm = pl.BlockSpec(memory_space=pltpu.HBM)
    return pl.pallas_call(
        lambda *refs: None,
        out_shape=jax.ShapeDtypeStruct(kept.shape, kept.dtype),
        in_specs=[hbm] * (1 + len(arrived)),
        out_specs=hbm,
        input_output_aliases={0: 0},
        compiler_params=pltpu.CompilerParams(vmem_limit_bytes=64 << 20),
        cost_estimate=pl.CostEstimate(flops=COVER, bytes_accessed=0, transcendentals=0),
        name="gate",
    )(kept, *arrived)


def write_edges(state, take, outs, chosen, rims, sides, marks, copies):
    values, first, second, rows, near = outs
    cx, cy, cz, lanes = state.shape
    rims[0] = state[0].astype(BF16)
    rims[1] = state[cx - 1].astype(BF16)
    for i in range(cx):
        sides[0, :, i * lanes : (i + 1) * lanes] = state[i, 0].astype(BF16)
        sides[1, :, i * lanes : (i + 1) * lanes] = state[i, cy - 1].astype(BF16)
    done = [
        copies.start(rims.at[1 - marks[0]], first),
        copies.start(rims.at[marks[0]], second),
        copies.start(sides, rows),
        copies.start(sides.at[1 - marks[1]], near),
    ]
    narrow = state[...].reshape(cx * cy * cz, lanes).astype(BF16)
    chosen[...] = matmul(take[...], narrow, ((1,), (0,))).astype(BF16)
    if values is not None:
        done.append(copies.start(chosen, values))
    return done


def edge_shapes(state, places):
    cx, cy, cz, lanes = state.shape
    return [
        jax.ShapeDtypeStruct((places, lanes), BF16),
        jax.ShapeDtypeStruct((cy, cz, lanes), BF16),
        jax.ShapeDtypeStruct((cy, cz, lanes), BF16),
        jax.ShapeDtypeStruct((2, cz, cx * lanes), BF16),
        jax.ShapeDtypeStruct((cz, cx * lanes), BF16),
    ]


def edge_scratch(state, places):
    cx, cy, cz, lanes = state.shape
    return [
        ((places, lanes), BF16),
        ((2, cy, cz, lanes), BF16),
        ((2, cz, cx * lanes), BF16),
    ]


def slot_places(bank_r):
    slots = bank_r.shape[1]
    down = lax.broadcasted_iota(jnp.int32, (slots, slots), 0)
    over = lax.broadcasted_iota(jnp.int32, (slots, slots), 1)

    def column(x):
        return jnp.sum(jnp.where(down == over, x, 0), axis=1, keepdims=True)

    bank_c = column(bank_r)
    same = bank_c == bank_r
    place_r = bank_r * CAP + jnp.sum(
        jnp.where(same & (down < over), 1, 0), axis=0, keepdims=True
    )
    return place_r, column(place_r), column


def first_panel(part):
    return lax.axis_index("bem") * part.shape[0]


def setup_body(*refs):
    marks = whereabouts()
    bank, cell, row, state, density, right = refs[:6]
    take, codes, sent = refs[6:9]
    outs = refs[9:13]
    banks_v, cells_v, rows_v, here, share_v, factor, picks, coded, packed = refs[13:22]
    chosen, rims, sides, sems = refs[22:]
    copies = Copies(sems)
    small = [copies.start(bank, banks_v), copies.start(cell, cells_v), copies.start(row, rows_v)]
    share = share_v.shape[0]
    start = pl.multiple_of(lax.axis_index("fem") * share, share)
    large = [
        copies.start(density.at[pl.ds(start, share)], share_v),
        copies.start(right.at[pl.ds(first_panel(factor), factor.shape[0])], factor),
        copies.start(state, here),
    ]
    for copy in small:
        copy.wait()
    slots = bank.shape[1]
    places, cells = take.shape
    banks, _, lanes = packed.shape
    cell_r = cells_v[...] + 1
    place_r, place_c, column = slot_places(banks_v[...])
    hit = lax.broadcasted_iota(jnp.int32, (places, slots), 0) == place_r
    cell_c = jnp.sum(jnp.where(hit, cell_r, 0), axis=1, keepdims=True)
    code = jnp.sum(jnp.where(hit, rows_v[...] + 1, 0), axis=1, keepdims=True)
    lane = lax.broadcasted_iota(jnp.int32, (places, lanes), 1)
    digits = jnp.where(lane == 0, code // 32, jnp.where(lane == 1, code % 32, 0))
    packed[:, CAP : 2 * CAP] = digits.astype(F32).astype(BF16).reshape(banks, CAP, lanes)
    ids = lax.broadcasted_iota(jnp.int32, (places, cells), 1) + 1
    picks[...] = (cell_c == ids).astype(F32).astype(BF16)
    out = [copies.start(picks, take)]
    hit = lax.broadcasted_iota(jnp.int32, (slots, places), 1) == place_c
    coded[...] = jnp.sum(jnp.where(hit, column(cell_r), 0), axis=0, keepdims=True)
    out.append(copies.start(coded, codes))
    for copy in large:
        copy.wait()
    out += write_edges(here, picks, (None, *outs), chosen, rims, sides, marks, copies)
    packed[:, :CAP] = chosen[...].reshape(banks, CAP, lanes)
    short = moments(share_v[...].astype(BF16), factor).astype(BF16)
    for k in range(banks):
        packed[k, 2 * CAP :] = short
    out.append(copies.start(packed, sent))
    for copy in out:
        copy.wait()


def setup_call(bank, cell, row, state, density, right, banks, share, per_dev):
    cx, cy, cz, lanes = state.shape
    slots = bank.shape[1]
    places = banks * CAP
    take = jax.ShapeDtypeStruct((places, cx * cy * cz), BF16)
    sent = (banks, 2 * CAP + share, lanes)
    return kernel_call(
        setup_body,
        [bank, cell, row, state, density, right],
        [
            take,
            jax.ShapeDtypeStruct((1, places), jnp.int32),
            jax.ShapeDtypeStruct(sent, BF16),
        ]
        + edge_shapes(state, places)[1:],
        [((1, slots), jnp.int32)] * 3
        + [
            (state.shape, F32),
            ((share, density.shape[1]), F32),
            ((per_dev, *right.shape[1:]), BF16),
            (take.shape, BF16),
            ((1, places), jnp.int32),
            (sent, BF16),
        ]
        + edge_scratch(state, places),
        13,
        2 * take.size * lanes,
        "setup",
    )


def moments(rounded, factor):
    per_dev, rank, rows = factor.shape
    sums = [
        matmul(rounded[:, q * rows : (q + 1) * rows], factor[q], ((1,), (1,)))
        for q in range(per_dev)
    ]
    sums.append(jnp.zeros((rounded.shape[0], 128 - per_dev * rank), F32))
    return jnp.concatenate(sums, axis=1)


def tables_body(codes, reaction, spread, inverse, codes_v, scale, wide, full, sems):
    copies = Copies(sems)
    for copy in [copies.start(codes, codes_v), copies.start(reaction, scale)]:
        copy.wait()
    wanted = codes_v[...]
    rows = 256
    for k in range(wide.shape[0] // rows):
        ids = lax.broadcasted_iota(jnp.int32, (rows, wanted.shape[1]), 0) + (k * rows + 1)
        wide[k * rows : (k + 1) * rows] = (ids == wanted).astype(F32).astype(BF16)
    done = [copies.start(wide, spread)]
    cx, cy, cz, lanes = full.shape
    scale[...] = 1.0 / (6.0 + scale[...])
    down = lax.broadcasted_iota(jnp.int32, (cz, cz), 0)
    over = lax.broadcasted_iota(jnp.int32, (cz, cz), 1)

    def plane(m, carry):
        i, j = m // cy, m % cy
        along_lanes = scale[i, pl.ds(j, 1), :]
        factor = jnp.sum(jnp.where(down == over, along_lanes, 0.0), axis=1, keepdims=True)
        full[i, j] = jnp.broadcast_to(factor, (cz, lanes))
        return carry

    lax.fori_loop(0, cx * cy, plane, 0, unroll=8)
    done.append(copies.start(full, inverse))
    for copy in done:
        copy.wait()


def tables_call(codes, reaction, lanes):
    spread = jax.ShapeDtypeStruct((reaction.size, codes.shape[1]), BF16)
    inverse = jax.ShapeDtypeStruct((*reaction.shape, lanes), F32)
    return kernel_call(
        tables_body,
        [codes, reaction],
        [spread, inverse],
        [
            (codes.shape, jnp.int32),
            (reaction.shape, F32),
            (spread.shape, BF16),
            (inverse.shape, F32),
        ],
        4,
        1 << 20,
        "tables",
    )


def weights_body(centers, pairs, weights, places, listed_v, mix, sems):
    copies = Copies(sems)
    for copy in [copies.start(centers, places), copies.start(pairs, listed_v)]:
        copy.wait()
    banks, per_dev, lanes = mix.shape
    panels = places.shape[1]
    rank = lanes // 2 // per_dev
    near = listed_v[...]
    ids = lax.broadcasted_iota(jnp.int32, (panels, near.shape[1]), 0)
    own = lax.broadcasted_iota(jnp.int32, (panels, 1), 0)
    panel = lax.broadcasted_iota(jnp.int32, (panels, lanes), 0)
    lane = lax.broadcasted_iota(jnp.int32, (panels, lanes), 1)
    spots = places[...]
    square = [lax.broadcasted_iota(jnp.int32, (panels, panels), d) for d in (0, 1)]
    which = lax.broadcasted_iota(jnp.int32, spots.shape, 1)
    own_first = lax.axis_index("bem") * per_dev
    for p in range(per_dev):
        here = jnp.sum(jnp.where(which == own_first + p, spots, 0.0), axis=1, keepdims=True)
        offset = here - spots
        apart = jnp.sum(offset * offset, axis=0, keepdims=True)
        apart = jnp.where(square[0] == square[1], apart, 0.0)
        kernel = 1.0 / (1.0 + jnp.sum(apart, axis=1, keepdims=True))
        hits = jnp.sum(jnp.where(ids == near[p : p + 1], 1, 0), axis=1, keepdims=True)
        kernel = jnp.where((hits > 0) | (own == own_first + p), 0.0, kernel)
        for k in range(banks):
            there = (panel == per_dev * k + lane // rank) & (lane < per_dev * rank)
            mix[k, p : p + 1] = jnp.sum(jnp.where(there, kernel, 0.0), axis=0, keepdims=True)
    copies.start(mix, weights).wait()


def weights_call(centers, pairs, banks):
    weights = jax.ShapeDtypeStruct((banks, pairs.shape[0], 128), F32)
    return kernel_call(
        weights_body,
        [centers, pairs],
        [weights],
        [(centers.shape, F32), (pairs.shape, jnp.int32), (weights.shape, F32)],
        3,
        1 << 20,
        "weights",
    )[0]


def fem_body(last, *refs):
    marks = whereabouts()
    state, source, inverse, spread, returned = refs[:5]
    first, second, near, inner, outer = refs[5:10]
    if last:
        out = refs[10]
        padded, load, scale, wide, back, rim, side, coupled, fresh, sems = refs[11:]
    else:
        take, out = refs[10:12]
        outs = refs[12:17]
        padded, load, scale, wide, back, rim, side, coupled, fresh = refs[17:26]
        picks, chosen, rims, sides, sems = refs[26:]
    cx, cy, cz, lanes = state.shape
    rows = inner.shape[0] - cz
    skip = CAP if returned.shape[1] > CAP else 0
    copies = Copies(sems)
    early = [copies.start(spread, wide), copies.start(returned.at[:, pl.ds(skip, CAP)], back)]
    late = [
        copies.start(first, rim.at[1 - marks[0]]),
        copies.start(second, rim.at[marks[0]]),
        copies.start(near, side.at[2]),
        copies.start(inner.at[pl.ds(rows, cz)], side.at[0]),
        copies.start(outer.at[pl.ds(rows, cz)], side.at[1]),
        copies.start(state, padded.at[pl.ds(1, cx), pl.ds(1, cy)]),
        copies.start(source, load),
        copies.start(inverse, scale),
    ]
    if not last:
        picking = copies.start(take, picks)
    for copy in early:
        copy.wait()
    coupled[...] = matmul(wide[...], back[...].reshape(-1, lanes), ((1,), (0,)))
    for copy in late:
        copy.wait()
    padded[0, 1 : cy + 1] = rim[0].astype(F32)
    padded[cx + 1, 1 : cy + 1] = rim[1].astype(F32)
    far, close = marks[1] * (cy + 1), (1 - marks[1]) * (cy + 1)
    held = jnp.full((cz, lanes), marks[4].astype(jnp.int32), jnp.int32) > 0
    for i in range(cx):
        part = side[marks[3], :, i * lanes : (i + 1) * lanes].astype(F32)
        padded[i + 1, far] = jnp.where(held, part, 0.0)
        padded[i + 1, close] = side[2, :, i * lanes : (i + 1) * lanes].astype(F32)
    depth = lax.broadcasted_iota(jnp.int32, (cz, lanes), 0)

    def plane(m, carry):
        i, j = m // cy, m % cy
        here = padded[i + 1, j + 1]
        beside = padded[i + 2, j + 1] + padded[i, j + 1]
        beside = beside + padded[i + 1, j + 2] + padded[i + 1, j]
        beside = beside + jnp.where(depth == cz - 1, 0.0, pltpu.roll(here, cz - 1, 0))
        beside = beside + jnp.where(depth == 0, 0.0, pltpu.roll(here, 1, 0))
        start = pl.multiple_of(m * cz, cz)
        value = load[i, j] + beside - coupled[pl.ds(start, cz), :]
        fresh[i, j] = value * scale[i, j]
        return carry

    lax.fori_loop(0, cx * cy, plane, 0, unroll=4)
    done = [copies.start(fresh, out)]
    if not last:
        picking.wait()
        done += write_edges(fresh, picks, outs, chosen, rims, sides, marks, copies)
    for copy in done:
        copy.wait()


def fem_call(state, source, inverse, spread, returned, halos, take, last):
    cx, cy, cz, lanes = state.shape
    outs = [jax.ShapeDtypeStruct(state.shape, F32)]
    ins = [state, source, inverse, spread, returned, *halos]
    scratch = [
        ((cx + 2, cy + 2, cz, lanes), F32),
        (state.shape, F32),
        (state.shape, F32),
        (spread.shape, BF16),
        ((returned.shape[0], CAP, lanes), BF16),
        ((2, cy, cz, lanes), BF16),
        ((3, cz, cx * lanes), BF16),
        ((cx * cy * cz, lanes), F32),
        (state.shape, F32),
    ]
    if not last:
        ins.append(take)
        outs += edge_shapes(state, take.shape[0])
        scratch += [(take.shape, BF16)] + edge_scratch(state, take.shape[0])
    return kernel_call(
        functools.partial(fem_body, last),
        ins,
        outs,
        scratch,
        17,
        4 * spread.size * lanes,
        "fem_last" if last else "fem_step",
    )


def share_of(whole, part, start):
    return whole if whole.shape == part.shape else whole.at[pl.ds(start, part.shape[0])]


def update_body(last, *refs):
    summed, density, source, diagonal = refs[:4]
    copies = None
    if last:
        out = refs[4]
        terms, here, load, scale, fresh, sems = refs[5:]
    else:
        right, out, spread, moment = refs[4:8]
        terms, here, load, scale, fresh, factor, narrow, short, sems = refs[8:]
    copies = Copies(sems)
    ins = [
        copies.start(summed, terms),
        copies.start(share_of(density, here, pl.multiple_of(lax.axis_index("fem") * here.shape[0], here.shape[0])), here),
        copies.start(share_of(source, load, pl.multiple_of(lax.axis_index("fem") * load.shape[0], load.shape[0])), load),
        copies.start(diagonal, scale),
    ]
    if not last:
        ins.append(copies.start(share_of(right, factor, first_panel(factor)), factor))
    for copy in ins:
        copy.wait()
    applied = jnp.sum(terms[...].astype(F32), axis=0)
    value = here[...] + (load[...] - applied) / scale[...]
    fresh[...] = value
    done = [copies.start(fresh, out)]
    if not last:
        rounded = value.astype(BF16)
        for k in range(narrow.shape[0]):
            narrow[k] = rounded
        done.append(copies.start(narrow, spread))
        short[...] = moments(rounded, factor).astype(BF16)
        done.append(copies.start(short, moment))
    for copy in done:
        copy.wait()


def update_call(summed, density, source, diagonal, right, per_dev, last):
    shape = summed.shape[1:]
    outs = [jax.ShapeDtypeStruct(shape, F32)]
    ins = [summed, density, source, diagonal]
    scratch = [
        (summed.shape, BF16),
        (shape, F32),
        (shape, F32),
        (diagonal.shape, F32),
        (shape, F32),
    ]
    if not last:
        ins.append(right)
        outs += [
            jax.ShapeDtypeStruct(summed.shape, BF16),
            jax.ShapeDtypeStruct((shape[0], 128), BF16),
        ]
        scratch += [
            ((per_dev, *right.shape[1:]), BF16),
            (summed.shape, BF16),
            ((shape[0], 128), BF16),
        ]
    return kernel_call(
        functools.partial(update_body, last),
        ins,
        outs,
        scratch,
        8,
        1 << 20,
        "update_last" if last else "update",
    )


def send_swaps(whole, sides, inner, outer, copies):
    height, cz = whole.shape[0], sides.shape[1]
    odd = whereabouts()[2]
    done = []
    for target, which in ((inner, 1 - odd), (outer, odd)):
        done.append(copies.start(whole, target.at[pl.ds(0, height)]))
        done.append(copies.start(sides.at[which], target.at[pl.ds(height, cz)]))
    return done


def load_body(density, rows, full, inner, outer, wide, whole, sides, sems):
    copies = Copies(sems)
    for copy in [copies.start(density, wide), copies.start(rows, sides)]:
        copy.wait()
    whole[...] = wide[...].astype(BF16)
    done = send_swaps(whole, sides, inner, outer, copies)
    done.append(copies.start(whole, full))
    for copy in done:
        copy.wait()


def load_call(density, rows):
    lanes, width = density.shape
    swap = jax.ShapeDtypeStruct((lanes + rows.shape[1], width), BF16)
    return kernel_call(
        load_body,
        [density, rows],
        [jax.ShapeDtypeStruct(density.shape, BF16), swap, swap],
        [(density.shape, F32), (density.shape, BF16), (rows.shape, BF16)],
        7,
        1 << 20,
        "load",
    )


def choose_body(received, full, hot, sent, coded, mask, whole, packed, sems):
    copies = Copies(sems)
    get = copies.start(received.at[:, pl.ds(CAP, CAP)], coded)
    load = copies.start(full, whole)
    get.wait()
    digits = coded[...].reshape(mask.shape[0], -1).astype(F32)
    code = (digits[:, :1] * 32.0 + digits[:, 1:2]).astype(jnp.int32)
    ids = lax.broadcasted_iota(jnp.int32, mask.shape, 1) + 1
    mask[...] = (code == ids).astype(F32).astype(BF16)
    done = [copies.start(mask, hot)]
    load.wait()
    picked = matmul(mask[...], whole[...], ((1,), (1,))).astype(BF16)
    packed[...] = picked.reshape(packed.shape)
    done.append(copies.start(packed, sent))
    for copy in done:
        copy.wait()


def choose_call(received, full):
    banks, _, lanes = received.shape
    mask = jax.ShapeDtypeStruct((banks * CAP, full.shape[1]), BF16)
    sent = jax.ShapeDtypeStruct((banks, CAP, lanes), BF16)
    return kernel_call(
        choose_body,
        [received, full],
        [mask, sent],
        [(sent.shape, BF16), (mask.shape, BF16), (full.shape, BF16), (sent.shape, BF16)],
        4,
        2 * mask.size * lanes,
        "choose",
    )


def pick_body(full, hot, values, moment, rows, sent, inner, outer, *refs):
    whole, mask, chosen, short, sides, packed, sems = refs
    copies = Copies(sems)
    ins = [
        copies.start(full, whole),
        copies.start(rows, sides),
        copies.start(values, chosen),
        copies.start(moment, short),
    ]
    get = copies.start(hot, mask)
    for copy in ins:
        copy.wait()
    done = send_swaps(whole, sides, inner, outer, copies)
    banks, lanes = packed.shape[0], packed.shape[2]
    packed[:, :CAP] = chosen[...].reshape(banks, CAP, lanes)
    for bank in range(banks):
        packed[bank, 2 * CAP :] = short[...]
    get.wait()
    picked = matmul(mask[...], whole[...], ((1,), (1,))).astype(BF16)
    packed[:, CAP : 2 * CAP] = picked.reshape(banks, CAP, lanes)
    done.append(copies.start(packed, sent))
    for copy in done:
        copy.wait()


def pick_call(full, hot, values, moment, rows, banks):
    lanes, width = full.shape
    sent = jax.ShapeDtypeStruct((banks, 2 * CAP + moment.shape[0], lanes), BF16)
    swap = jax.ShapeDtypeStruct((lanes + rows.shape[1], width), BF16)
    ins = [full, hot, values, moment, rows]
    return kernel_call(
        pick_body,
        ins,
        [sent, swap, swap],
        [(x.shape, BF16) for x in (*ins, sent)],
        10,
        2 * hot.size * lanes,
        "pick",
    )


def exchange(x, axis):
    return lax.all_to_all(x, axis, split_axis=0, concat_axis=0, tiled=True)


def swaps(x_first, x_second, axis):
    size = lax.axis_size(axis)
    inner = [(i, i ^ 1) for i in range(size)]
    outer = [(i, i + 1) if i % 2 else (i, i - 1) for i in range(1, size - 1)]
    return lax.ppermute(x_first, axis, inner), lax.ppermute(x_second, axis, outer)


def chip_swaps(x_inner, x_outer, axis):
    size = lax.axis_size(axis)
    inner = [(i, i ^ 2) for i in range(size)]
    outer = [(i, (i + 2 if i // 2 % 2 else i - 2) % size) for i in range(size)]
    return lax.ppermute(x_inner, axis, inner), lax.ppermute(x_outer, axis, outer)


def ordered(x, *others):
    return lax.optimization_barrier((x, others))[0]


def partner(x, axis):
    return lax.ppermute(x, axis, [(i, i ^ 1) for i in range(lax.axis_size(axis))])


def shards(
    fem_field,
    fem_source,
    reaction,
    bem_density,
    bem_source,
    bem_diagonal,
    near_blocks,
    near_pairs,
    low_left,
    low_right,
    centers,
    trace_cell,
    trace_bank,
    trace_row,
):
    fem_count = lax.axis_size("fem")
    bem_count = lax.axis_size("bem")
    excitations, local_rows = bem_density.shape
    share = excitations // fem_count
    per_dev, group, panel_rows, _ = near_blocks.shape
    bank = trace_bank.reshape(1, -1)
    take, codes, sent, *edges = setup_call(
        bank,
        trace_cell.reshape(1, -1),
        trace_row.reshape(1, -1),
        fem_field,
        bem_density,
        low_right,
        bem_count,
        share,
        per_dev,
    )
    weights = weights_call(centers.T, near_pairs, bem_count)
    diag_row = bem_diagonal[None, :]

    fem_state, density = fem_field, bem_density
    for sweep in range(ITERS):
        initial, last = sweep == 0, sweep == ITERS - 1
        first, second, rows, near = edges
        if initial:
            full, inner, outer = load_call(bem_density, rows)
            first, second, near = ordered((first, second, near), full)
        else:
            full = exchange(copies, "fem").reshape(excitations, local_rows)
            full = ordered(full, values)
            sent, inner, outer = pick_call(full, hot, values, moment, rows, bem_count)
            first, second, near = ordered((first, second, near), sent)
        inner, outer = chip_swaps(inner, outer, "bem")
        received = returned = exchange(sent, "bem")
        if initial:
            hot, picked = choose_call(received, full)
        others = [partner(x, "bem") for x in (inner, full, outer)]
        parts = [inner, others[0], full, others[1], outer, others[2]]
        if initial:
            returned = exchange(picked, "bem")
        halos = swaps(first, second, "fem") + (partner(near, "bem"),)
        weights = gate_call(weights, received, *halos)
        partial = near_call(near_pairs, parts, near_blocks, received, hot, weights, low_left)
        if initial:
            partial = ordered(partial, returned)
        summed = exchange(partial.reshape(fem_count, share, local_rows), "fem")

        def fem_step(after):
            return fem_call(
                ordered(fem_state, after),
                fem_source,
                inverse,
                spread,
                returned,
                (*halos, others[0], others[2]),
                take,
                last,
            )

        if initial:
            spread, inverse = tables_call(ordered(codes, partial), reaction, excitations)
            summed = ordered(summed, spread)
        else:
            fem_state, *rest = fem_step(partial)
            summed = ordered(summed, fem_state)
        density, *more = update_call(
            summed, density, bem_source, diag_row, low_right, per_dev, last
        )
        if not last:
            copies, moment = more
        if initial:
            fem_state, *rest = fem_step(copies)
        if not last:
            values, *edges = rest
    return (fem_state, density)


def solution(mesh):
    return jax.shard_map(
        shards,
        mesh=mesh,
        in_specs=(
            P("fem", "bem", None, None),
            P("fem", "bem", None, None),
            P("fem", "bem", None),
            P(None, "bem"),
            P(None, "bem"),
            P("bem"),
            P("bem", "fem", None, None),
            P("bem", None),
            P("bem", None, None),
            P(),
            P(),
            P(("fem", "bem")),
            P(("fem", "bem"), None),
            P(("fem", "bem")),
        ),
        out_specs=(P("fem", "bem", None, None), P("fem", "bem")),
        check_vma=False,
    )
```

```python
import functools

import jax
import jax.numpy as jnp
from jax import lax
from jax.experimental import pallas as pl
from jax.experimental.pallas import tpu as pltpu
from jax.sharding import PartitionSpec as P

CAP = 32
ITERS = 3
COVER = 20_000_000_000
HIGHEST = lax.Precision.HIGHEST
BF16 = jnp.bfloat16
F32 = jnp.float32


def matmul(left, right, dims):
    return lax.dot_general(left, right, (dims, ((), ())), preferred_element_type=F32)


def kernel_call(body, args, outs, scratch, copies, flops, name, smem=()):
    hbm = pl.BlockSpec(memory_space=pltpu.HBM)
    scalar = pl.BlockSpec(memory_space=pltpu.SMEM)
    args = [*smem, *args]
    return pl.pallas_call(
        body,
        out_shape=outs,
        in_specs=[scalar] * len(smem) + [hbm] * (len(args) - len(smem)),
        out_specs=[hbm] * len(outs),
        scratch_shapes=[pltpu.VMEM(s, t) for s, t in scratch] + [pltpu.SemaphoreType.DMA((copies,))],
        compiler_params=pltpu.CompilerParams(vmem_limit_bytes=64 << 20),
        cost_estimate=pl.CostEstimate(
            flops=flops,
            bytes_accessed=sum(x.size * x.dtype.itemsize for x in args),
            transcendentals=0,
        ),
        name=name,
    )(*args)


class Copies:
    def __init__(self, sems):
        self.sems, self.count = sems, 0

    def start(self, source, target):
        copy = pltpu.make_async_copy(source, target, self.sems.at[self.count])
        self.count += 1
        copy.start()
        return copy


def whereabouts():
    bem = lax.axis_index("bem")
    core, odd = bem % 2, bem // 2 % 2
    inside = (bem > 0) & (bem < lax.axis_size("bem") - 1)
    return (lax.axis_index("fem") % 2, core, odd, (core + odd + 1) % 2, inside)


def near_body(pairs, *refs):
    parts = refs[:6]
    blocks, received, hot, weights, factors, out = refs[6:12]
    panels, held, got, mask, mix, factor, total, narrow, sems = refs[12:]
    per_dev, group, rows, _ = blocks.shape
    share = panels.shape[1] // lax.axis_size("fem")
    rank = factors.shape[1]
    copies = Copies(sems)
    small = [
        copies.start(received, got),
        copies.start(hot, mask),
        copies.start(weights, mix),
    ]
    for k in range(per_dev):
        small.append(copies.start(factors, factor.at[:, k * rank : (k + 1) * rank]))
    moved = []
    for place, ref in enumerate(parts):
        for half in range(per_dev):
            moved.append(
                copies.start(
                    ref.at[pl.ds(0, panels.shape[1]), half * rows : (half + 1) * rows],
                    panels.at[place * per_dev + half],
                )
            )
    loads = []
    for half in range(per_dev):
        for step in range(group):
            loads.append(copies.start(blocks.at[half, step], held.at[half * group + step]))
    factor[:, per_dev * rank :] = jnp.zeros_like(factor[:, per_dev * rank :])
    for copy in small:
        copy.wait()
    fem, bem, banks = lax.axis_index("fem"), lax.axis_index("bem"), lax.axis_size("bem")
    values = got[:, :CAP, :].reshape(-1, got.shape[2])
    traced = matmul(values, mask[...], ((0,), (0,)))
    start = pl.multiple_of(fem * share, share)
    for half in range(per_dev):
        mixed = jnp.zeros((share, got.shape[2]), F32)
        for bank in range(got.shape[0]):
            mixed = mixed + mix[bank, half : half + 1, :] * got[
                bank, got.shape[1] - share :, :
            ].astype(F32)
        upper = mixed.astype(BF16)
        lower = (mixed - upper.astype(F32)).astype(BF16)
        far = matmul(upper, factor[half], ((1,), (0,))) + matmul(lower, factor[half], ((1,), (0,)))
        total[half] = traced[:, half * rows : (half + 1) * rows]
        total[half, pl.ds(start, share), :] += far
    for copy in moved:
        copy.wait()
    done = []
    for half in range(per_dev):
        summed = total[half]
        for step in range(group):
            source = pairs[half, fem * group + step]
            bank = source // per_dev
            chip = (bank // 2 - bem // 2 + 1 + banks // 2) % (banks // 2)
            chip = jnp.where(bem // 2 % 2 == 1, chip, 2 - chip)
            place = (chip * 2 + (bank + bem) % 2) * per_dev + source % per_dev
            loads[half * group + step].wait()
            summed = summed + matmul(panels[place], held[half * group + step], ((1,), (0,)))
        narrow[half] = summed.astype(BF16)
        done.append(copies.start(narrow.at[half], out.at[:, half * rows : (half + 1) * rows]))
    for copy in done:
        copy.wait()


def near_call(pairs, parts, near_blocks, received, hot, weights, factors):
    per_dev, group, rows, _ = near_blocks.shape
    excitations = parts[2].shape[0]
    return kernel_call(
        near_body,
        [*parts, near_blocks, received, hot, weights, factors],
        [jax.ShapeDtypeStruct((excitations, per_dev * rows), BF16)],
        [
            ((6 * per_dev, excitations, rows), BF16),
            ((per_dev * group, rows, rows), BF16),
            (received.shape, BF16),
            (hot.shape, BF16),
            (weights.shape, F32),
            ((per_dev, weights.shape[2], rows), BF16),
            ((per_dev, excitations, rows), F32),
            ((per_dev, excitations, rows), BF16),
        ],
        3 + per_dev + 6 * per_dev + per_dev * group + per_dev,
        2 * excitations * near_blocks.size // rows * rows,
        "near",
        smem=[pairs],
    )[0]


def gate_call(kept, *arrived):
    hbm = pl.BlockSpec(memory_space=pltpu.HBM)
    return pl.pallas_call(
        lambda *refs: None,
        out_shape=jax.ShapeDtypeStruct(kept.shape, kept.dtype),
        in_specs=[hbm] * (1 + len(arrived)),
        out_specs=hbm,
        input_output_aliases={0: 0},
        compiler_params=pltpu.CompilerParams(vmem_limit_bytes=64 << 20),
        cost_estimate=pl.CostEstimate(flops=COVER, bytes_accessed=0, transcendentals=0),
        name="gate",
    )(kept, *arrived)


def write_edges(state, take, outs, chosen, rims, sides, marks, copies):
    values, first, second, rows, near = outs
    cx, cy, cz, lanes = state.shape
    rims[0] = state[0].astype(BF16)
    rims[1] = state[cx - 1].astype(BF16)
    for i in range(cx):
        sides[0, :, i * lanes : (i + 1) * lanes] = state[i, 0].astype(BF16)
        sides[1, :, i * lanes : (i + 1) * lanes] = state[i, cy - 1].astype(BF16)
    done = [
        copies.start(rims.at[1 - marks[0]], first),
        copies.start(rims.at[marks[0]], second),
        copies.start(sides, rows),
        copies.start(sides.at[1 - marks[1]], near),
    ]
    narrow = state[...].reshape(cx * cy * cz, lanes).astype(BF16)
    chosen[...] = matmul(take[...], narrow, ((1,), (0,))).astype(BF16)
    if values is not None:
        done.append(copies.start(chosen, values))
    return done


def edge_shapes(state, places):
    cx, cy, cz, lanes = state.shape
    return [
        jax.ShapeDtypeStruct((places, lanes), BF16),
        jax.ShapeDtypeStruct((cy, cz, lanes), BF16),
        jax.ShapeDtypeStruct((cy, cz, lanes), BF16),
        jax.ShapeDtypeStruct((2, cz, cx * lanes), BF16),
        jax.ShapeDtypeStruct((cz, cx * lanes), BF16),
    ]


def edge_scratch(state, places):
    cx, cy, cz, lanes = state.shape
    return [
        ((places, lanes), BF16),
        ((2, cy, cz, lanes), BF16),
        ((2, cz, cx * lanes), BF16),
    ]


def slot_places(bank_r):
    slots = bank_r.shape[1]
    down = lax.broadcasted_iota(jnp.int32, (slots, slots), 0)
    over = lax.broadcasted_iota(jnp.int32, (slots, slots), 1)

    def column(x):
        return jnp.sum(jnp.where(down == over, x, 0), axis=1, keepdims=True)

    bank_c = column(bank_r)
    same = bank_c == bank_r
    place_r = bank_r * CAP + jnp.sum(
        jnp.where(same & (down < over), 1, 0), axis=0, keepdims=True
    )
    return place_r, column(place_r), column


def first_panel(part):
    return lax.axis_index("bem") * part.shape[0]


def setup_body(*refs):
    marks = whereabouts()
    bank, cell, row, state, density, right = refs[:6]
    take, codes, sent = refs[6:9]
    outs = refs[9:13]
    banks_v, cells_v, rows_v, here, share_v, factor, picks, coded, packed = refs[13:22]
    chosen, rims, sides, sems = refs[22:]
    copies = Copies(sems)
    small = [copies.start(bank, banks_v), copies.start(cell, cells_v), copies.start(row, rows_v)]
    share = share_v.shape[0]
    start = pl.multiple_of(lax.axis_index("fem") * share, share)
    large = [
        copies.start(density.at[pl.ds(start, share)], share_v),
        copies.start(right.at[pl.ds(first_panel(factor), factor.shape[0])], factor),
        copies.start(state, here),
    ]
    for copy in small:
        copy.wait()
    slots = bank.shape[1]
    places, cells = take.shape
    banks, _, lanes = packed.shape
    cell_r = cells_v[...] + 1
    place_r, place_c, column = slot_places(banks_v[...])
    hit = lax.broadcasted_iota(jnp.int32, (places, slots), 0) == place_r
    cell_c = jnp.sum(jnp.where(hit, cell_r, 0), axis=1, keepdims=True)
    code = jnp.sum(jnp.where(hit, rows_v[...] + 1, 0), axis=1, keepdims=True)
    lane = lax.broadcasted_iota(jnp.int32, (places, lanes), 1)
    digits = jnp.where(lane == 0, code // 32, jnp.where(lane == 1, code % 32, 0))
    packed[:, CAP : 2 * CAP] = digits.astype(F32).astype(BF16).reshape(banks, CAP, lanes)
    ids = lax.broadcasted_iota(jnp.int32, (places, cells), 1) + 1
    picks[...] = (cell_c == ids).astype(F32).astype(BF16)
    out = [copies.start(picks, take)]
    hit = lax.broadcasted_iota(jnp.int32, (slots, places), 1) == place_c
    coded[...] = jnp.sum(jnp.where(hit, column(cell_r), 0), axis=0, keepdims=True)
    out.append(copies.start(coded, codes))
    for copy in large:
        copy.wait()
    out += write_edges(here, picks, (None, *outs), chosen, rims, sides, marks, copies)
    packed[:, :CAP] = chosen[...].reshape(banks, CAP, lanes)
    short = moments(share_v[...].astype(BF16), factor).astype(BF16)
    for k in range(banks):
        packed[k, 2 * CAP :] = short
    out.append(copies.start(packed, sent))
    for copy in out:
        copy.wait()


def setup_call(bank, cell, row, state, density, right, banks, share, per_dev):
    cx, cy, cz, lanes = state.shape
    slots = bank.shape[1]
    places = banks * CAP
    take = jax.ShapeDtypeStruct((places, cx * cy * cz), BF16)
    sent = (banks, 2 * CAP + share, lanes)
    return kernel_call(
        setup_body,
        [bank, cell, row, state, density, right],
        [
            take,
            jax.ShapeDtypeStruct((1, places), jnp.int32),
            jax.ShapeDtypeStruct(sent, BF16),
        ]
        + edge_shapes(state, places)[1:],
        [((1, slots), jnp.int32)] * 3
        + [
            (state.shape, F32),
            ((share, density.shape[1]), F32),
            ((per_dev, *right.shape[1:]), BF16),
            (take.shape, BF16),
            ((1, places), jnp.int32),
            (sent, BF16),
        ]
        + edge_scratch(state, places),
        13,
        2 * take.size * lanes,
        "setup",
    )


def moments(rounded, factor):
    per_dev, rank, rows = factor.shape
    sums = [
        matmul(rounded[:, q * rows : (q + 1) * rows], factor[q], ((1,), (1,)))
        for q in range(per_dev)
    ]
    sums.append(jnp.zeros((rounded.shape[0], 128 - per_dev * rank), F32))
    return jnp.concatenate(sums, axis=1)


def tables_body(codes, reaction, spread, inverse, codes_v, scale, wide, full, sems):
    copies = Copies(sems)
    for copy in [copies.start(codes, codes_v), copies.start(reaction, scale)]:
        copy.wait()
    wanted = codes_v[...]
    rows = 256
    for k in range(wide.shape[0] // rows):
        ids = lax.broadcasted_iota(jnp.int32, (rows, wanted.shape[1]), 0) + (k * rows + 1)
        wide[k * rows : (k + 1) * rows] = (ids == wanted).astype(F32).astype(BF16)
    done = [copies.start(wide, spread)]
    cx, cy, cz, lanes = full.shape
    scale[...] = 1.0 / (6.0 + scale[...])
    down = lax.broadcasted_iota(jnp.int32, (cz, cz), 0)
    over = lax.broadcasted_iota(jnp.int32, (cz, cz), 1)

    def plane(m, carry):
        i, j = m // cy, m % cy
        along_lanes = scale[i, pl.ds(j, 1), :]
        factor = jnp.sum(jnp.where(down == over, along_lanes, 0.0), axis=1, keepdims=True)
        full[i, j] = jnp.broadcast_to(factor, (cz, lanes))
        return carry

    lax.fori_loop(0, cx * cy, plane, 0, unroll=8)
    done.append(copies.start(full, inverse))
    for copy in done:
        copy.wait()


def tables_call(codes, reaction, lanes):
    spread = jax.ShapeDtypeStruct((reaction.size, codes.shape[1]), BF16)
    inverse = jax.ShapeDtypeStruct((*reaction.shape, lanes), F32)
    return kernel_call(
        tables_body,
        [codes, reaction],
        [spread, inverse],
        [
            (codes.shape, jnp.int32),
            (reaction.shape, F32),
            (spread.shape, BF16),
            (inverse.shape, F32),
        ],
        4,
        1 << 20,
        "tables",
    )


def weights_body(centers, pairs, weights, places, listed_v, mix, sems):
    copies = Copies(sems)
    for copy in [copies.start(centers, places), copies.start(pairs, listed_v)]:
        copy.wait()
    banks, per_dev, lanes = mix.shape
    panels = places.shape[1]
    rank = lanes // 2 // per_dev
    near = listed_v[...]
    ids = lax.broadcasted_iota(jnp.int32, (panels, near.shape[1]), 0)
    own = lax.broadcasted_iota(jnp.int32, (panels, 1), 0)
    panel = lax.broadcasted_iota(jnp.int32, (panels, lanes), 0)
    lane = lax.broadcasted_iota(jnp.int32, (panels, lanes), 1)
    spots = places[...]
    square = [lax.broadcasted_iota(jnp.int32, (panels, panels), d) for d in (0, 1)]
    which = lax.broadcasted_iota(jnp.int32, spots.shape, 1)
    own_first = lax.axis_index("bem") * per_dev
    for p in range(per_dev):
        here = jnp.sum(jnp.where(which == own_first + p, spots, 0.0), axis=1, keepdims=True)
        offset = here - spots
        apart = jnp.sum(offset * offset, axis=0, keepdims=True)
        apart = jnp.where(square[0] == square[1], apart, 0.0)
        kernel = 1.0 / (1.0 + jnp.sum(apart, axis=1, keepdims=True))
        hits = jnp.sum(jnp.where(ids == near[p : p + 1], 1, 0), axis=1, keepdims=True)
        kernel = jnp.where((hits > 0) | (own == own_first + p), 0.0, kernel)
        for k in range(banks):
            there = (panel == per_dev * k + lane // rank) & (lane < per_dev * rank)
            mix[k, p : p + 1] = jnp.sum(jnp.where(there, kernel, 0.0), axis=0, keepdims=True)
    copies.start(mix, weights).wait()


def weights_call(centers, pairs, banks):
    weights = jax.ShapeDtypeStruct((banks, pairs.shape[0], 128), F32)
    return kernel_call(
        weights_body,
        [centers, pairs],
        [weights],
        [(centers.shape, F32), (pairs.shape, jnp.int32), (weights.shape, F32)],
        3,
        1 << 20,
        "weights",
    )[0]


def fem_body(last, *refs):
    marks = whereabouts()
    state, source, inverse, spread, returned = refs[:5]
    first, second, near, inner, outer = refs[5:10]
    if last:
        out = refs[10]
        padded, load, scale, wide, back, rim, side, coupled, fresh, sems = refs[11:]
    else:
        take, out = refs[10:12]
        outs = refs[12:17]
        padded, load, scale, wide, back, rim, side, coupled, fresh = refs[17:26]
        picks, chosen, rims, sides, sems = refs[26:]
    cx, cy, cz, lanes = state.shape
    rows = inner.shape[0] - cz
    skip = CAP if returned.shape[1] > CAP else 0
    copies = Copies(sems)
    early = [copies.start(spread, wide), copies.start(returned.at[:, pl.ds(skip, CAP)], back)]
    late = [
        copies.start(first, rim.at[1 - marks[0]]),
        copies.start(second, rim.at[marks[0]]),
        copies.start(near, side.at[2]),
        copies.start(inner.at[pl.ds(rows, cz)], side.at[0]),
        copies.start(outer.at[pl.ds(rows, cz)], side.at[1]),
        copies.start(state, padded.at[pl.ds(1, cx), pl.ds(1, cy)]),
        copies.start(source, load),
        copies.start(inverse, scale),
    ]
    if not last:
        picking = copies.start(take, picks)
    for copy in early:
        copy.wait()
    coupled[...] = matmul(wide[...], back[...].reshape(-1, lanes), ((1,), (0,)))
    for copy in late:
        copy.wait()
    padded[0, 1 : cy + 1] = rim[0].astype(F32)
    padded[cx + 1, 1 : cy + 1] = rim[1].astype(F32)
    far, close = marks[1] * (cy + 1), (1 - marks[1]) * (cy + 1)
    held = jnp.full((cz, lanes), marks[4].astype(jnp.int32), jnp.int32) > 0
    for i in range(cx):
        part = side[marks[3], :, i * lanes : (i + 1) * lanes].astype(F32)
        padded[i + 1, far] = jnp.where(held, part, 0.0)
        padded[i + 1, close] = side[2, :, i * lanes : (i + 1) * lanes].astype(F32)
    depth = lax.broadcasted_iota(jnp.int32, (cz, lanes), 0)

    def plane(m, carry):
        i, j = m // cy, m % cy
        here = padded[i + 1, j + 1]
        beside = padded[i + 2, j + 1] + padded[i, j + 1]
        beside = beside + padded[i + 1, j + 2] + padded[i + 1, j]
        beside = beside + jnp.where(depth == cz - 1, 0.0, pltpu.roll(here, cz - 1, 0))
        beside = beside + jnp.where(depth == 0, 0.0, pltpu.roll(here, 1, 0))
        start = pl.multiple_of(m * cz, cz)
        value = load[i, j] + beside - coupled[pl.ds(start, cz), :]
        fresh[i, j] = value * scale[i, j]
        return carry

    lax.fori_loop(0, cx * cy, plane, 0, unroll=4)
    done = [copies.start(fresh, out)]
    if not last:
        picking.wait()
        done += write_edges(fresh, picks, outs, chosen, rims, sides, marks, copies)
    for copy in done:
        copy.wait()


def fem_call(state, source, inverse, spread, returned, halos, take, last):
    cx, cy, cz, lanes = state.shape
    outs = [jax.ShapeDtypeStruct(state.shape, F32)]
    ins = [state, source, inverse, spread, returned, *halos]
    scratch = [
        ((cx + 2, cy + 2, cz, lanes), F32),
        (state.shape, F32),
        (state.shape, F32),
        (spread.shape, BF16),
        ((returned.shape[0], CAP, lanes), BF16),
        ((2, cy, cz, lanes), BF16),
        ((3, cz, cx * lanes), BF16),
        ((cx * cy * cz, lanes), F32),
        (state.shape, F32),
    ]
    if not last:
        ins.append(take)
        outs += edge_shapes(state, take.shape[0])
        scratch += [(take.shape, BF16)] + edge_scratch(state, take.shape[0])
    return kernel_call(
        functools.partial(fem_body, last),
        ins,
        outs,
        scratch,
        17,
        4 * spread.size * lanes,
        "fem_last" if last else "fem_step",
    )


def share_of(whole, part, start):
    return whole if whole.shape == part.shape else whole.at[pl.ds(start, part.shape[0])]


def update_body(last, *refs):
    summed, density, source, diagonal = refs[:4]
    copies = None
    if last:
        out = refs[4]
        terms, here, load, scale, fresh, sems = refs[5:]
    else:
        right, out, spread, moment = refs[4:8]
        terms, here, load, scale, fresh, factor, narrow, short, sems = refs[8:]
    copies = Copies(sems)
    ins = [
        copies.start(summed, terms),
        copies.start(share_of(density, here, pl.multiple_of(lax.axis_index("fem") * here.shape[0], here.shape[0])), here),
        copies.start(share_of(source, load, pl.multiple_of(lax.axis_index("fem") * load.shape[0], load.shape[0])), load),
        copies.start(diagonal, scale),
    ]
    if not last:
        ins.append(copies.start(share_of(right, factor, first_panel(factor)), factor))
    for copy in ins:
        copy.wait()
    applied = jnp.sum(terms[...].astype(F32), axis=0)
    value = here[...] + (load[...] - applied) / scale[...]
    fresh[...] = value
    done = [copies.start(fresh, out)]
    if not last:
        rounded = value.astype(BF16)
        for k in range(narrow.shape[0]):
            narrow[k] = rounded
        done.append(copies.start(narrow, spread))
        short[...] = moments(rounded, factor).astype(BF16)
        done.append(copies.start(short, moment))
    for copy in done:
        copy.wait()


def update_call(summed, density, source, diagonal, right, per_dev, last):
    shape = summed.shape[1:]
    outs = [jax.ShapeDtypeStruct(shape, F32)]
    ins = [summed, density, source, diagonal]
    scratch = [
        (summed.shape, BF16),
        (shape, F32),
        (shape, F32),
        (diagonal.shape, F32),
        (shape, F32),
    ]
    if not last:
        ins.append(right)
        outs += [
            jax.ShapeDtypeStruct(summed.shape, BF16),
            jax.ShapeDtypeStruct((shape[0], 128), BF16),
        ]
        scratch += [
            ((per_dev, *right.shape[1:]), BF16),
            (summed.shape, BF16),
            ((shape[0], 128), BF16),
        ]
    return kernel_call(
        functools.partial(update_body, last),
        ins,
        outs,
        scratch,
        8,
        1 << 20,
        "update_last" if last else "update",
    )


def send_swaps(whole, sides, inner, outer, copies):
    height, cz = whole.shape[0], sides.shape[1]
    odd = whereabouts()[2]
    done = []
    for target, which in ((inner, 1 - odd), (outer, odd)):
        done.append(copies.start(whole, target.at[pl.ds(0, height)]))
        done.append(copies.start(sides.at[which], target.at[pl.ds(height, cz)]))
    return done


def load_body(density, rows, full, inner, outer, wide, whole, sides, sems):
    copies = Copies(sems)
    for copy in [copies.start(density, wide), copies.start(rows, sides)]:
        copy.wait()
    whole[...] = wide[...].astype(BF16)
    done = send_swaps(whole, sides, inner, outer, copies)
    done.append(copies.start(whole, full))
    for copy in done:
        copy.wait()


def load_call(density, rows):
    lanes, width = density.shape
    swap = jax.ShapeDtypeStruct((lanes + rows.shape[1], width), BF16)
    return kernel_call(
        load_body,
        [density, rows],
        [jax.ShapeDtypeStruct(density.shape, BF16), swap, swap],
        [(density.shape, F32), (density.shape, BF16), (rows.shape, BF16)],
        7,
        COVER,
        "load",
    )


def choose_body(received, full, hot, sent, coded, mask, whole, packed, sems):
    copies = Copies(sems)
    get = copies.start(received.at[:, pl.ds(CAP, CAP)], coded)
    load = copies.start(full, whole)
    get.wait()
    digits = coded[...].reshape(mask.shape[0], -1).astype(F32)
    code = (digits[:, :1] * 32.0 + digits[:, 1:2]).astype(jnp.int32)
    ids = lax.broadcasted_iota(jnp.int32, mask.shape, 1) + 1
    mask[...] = (code == ids).astype(F32).astype(BF16)
    done = [copies.start(mask, hot)]
    load.wait()
    picked = matmul(mask[...], whole[...], ((1,), (1,))).astype(BF16)
    packed[...] = picked.reshape(packed.shape)
    done.append(copies.start(packed, sent))
    for copy in done:
        copy.wait()


def choose_call(received, full):
    banks, _, lanes = received.shape
    mask = jax.ShapeDtypeStruct((banks * CAP, full.shape[1]), BF16)
    sent = jax.ShapeDtypeStruct((banks, CAP, lanes), BF16)
    return kernel_call(
        choose_body,
        [received, full],
        [mask, sent],
        [(sent.shape, BF16), (mask.shape, BF16), (full.shape, BF16), (sent.shape, BF16)],
        4,
        2 * mask.size * lanes,
        "choose",
    )


def pick_body(full, hot, values, moment, rows, sent, inner, outer, *refs):
    whole, mask, chosen, short, sides, packed, sems = refs
    copies = Copies(sems)
    ins = [
        copies.start(full, whole),
        copies.start(rows, sides),
        copies.start(values, chosen),
        copies.start(moment, short),
    ]
    get = copies.start(hot, mask)
    for copy in ins:
        copy.wait()
    done = send_swaps(whole, sides, inner, outer, copies)
    banks, lanes = packed.shape[0], packed.shape[2]
    packed[:, :CAP] = chosen[...].reshape(banks, CAP, lanes)
    for bank in range(banks):
        packed[bank, 2 * CAP :] = short[...]
    get.wait()
    picked = matmul(mask[...], whole[...], ((1,), (1,))).astype(BF16)
    packed[:, CAP : 2 * CAP] = picked.reshape(banks, CAP, lanes)
    done.append(copies.start(packed, sent))
    for copy in done:
        copy.wait()


def pick_call(full, hot, values, moment, rows, banks):
    lanes, width = full.shape
    sent = jax.ShapeDtypeStruct((banks, 2 * CAP + moment.shape[0], lanes), BF16)
    swap = jax.ShapeDtypeStruct((lanes + rows.shape[1], width), BF16)
    ins = [full, hot, values, moment, rows]
    return kernel_call(
        pick_body,
        ins,
        [sent, swap, swap],
        [(x.shape, BF16) for x in (*ins, sent)],
        10,
        2 * hot.size * lanes,
        "pick",
    )


def exchange(x, axis):
    return lax.all_to_all(x, axis, split_axis=0, concat_axis=0, tiled=True)


def swaps(x_first, x_second, axis):
    size = lax.axis_size(axis)
    inner = [(i, i ^ 1) for i in range(size)]
    outer = [(i, i + 1) if i % 2 else (i, i - 1) for i in range(1, size - 1)]
    return lax.ppermute(x_first, axis, inner), lax.ppermute(x_second, axis, outer)


def chip_swaps(x_inner, x_outer, axis):
    size = lax.axis_size(axis)
    inner = [(i, i ^ 2) for i in range(size)]
    outer = [(i, (i + 2 if i // 2 % 2 else i - 2) % size) for i in range(size)]
    return lax.ppermute(x_inner, axis, inner), lax.ppermute(x_outer, axis, outer)


def ordered(x, *others):
    return lax.optimization_barrier((x, others))[0]


def partner(x, axis):
    return lax.ppermute(x, axis, [(i, i ^ 1) for i in range(lax.axis_size(axis))])


def shards(
    fem_field,
    fem_source,
    reaction,
    bem_density,
    bem_source,
    bem_diagonal,
    near_blocks,
    near_pairs,
    low_left,
    low_right,
    centers,
    trace_cell,
    trace_bank,
    trace_row,
):
    fem_count = lax.axis_size("fem")
    bem_count = lax.axis_size("bem")
    excitations, local_rows = bem_density.shape
    share = excitations // fem_count
    per_dev, group, panel_rows, _ = near_blocks.shape
    bank = trace_bank.reshape(1, -1)
    take, codes, sent, *edges = setup_call(
        bank,
        trace_cell.reshape(1, -1),
        trace_row.reshape(1, -1),
        fem_field,
        bem_density,
        low_right,
        bem_count,
        share,
        per_dev,
    )
    diag_row = bem_diagonal[None, :]

    fem_state, density = fem_field, bem_density
    for sweep in range(ITERS):
        initial, last = sweep == 0, sweep == ITERS - 1
        first, second, rows, near = edges
        if initial:
            full, inner, outer = load_call(bem_density, rows)
        else:
            full = exchange(copies, "fem").reshape(excitations, local_rows)
            full = ordered(full, values)
            sent, inner, outer = pick_call(full, hot, values, moment, rows, bem_count)
            first, second, near = ordered((first, second, near), sent)
        inner, outer = chip_swaps(inner, outer, "bem")
        received = returned = exchange(sent, "bem")
        if initial:
            hot, picked = choose_call(received, full)
            first, second, near = ordered((first, second, near), picked)
            weights = weights_call(ordered(centers.T, picked), near_pairs, bem_count)
        others = [partner(x, "bem") for x in (inner, full, outer)]
        parts = [inner, others[0], full, others[1], outer, others[2]]
        if initial:
            returned = exchange(picked, "bem")
        halos = swaps(first, second, "fem") + (partner(near, "bem"),)
        weights = gate_call(weights, received, *halos)
        partial = near_call(near_pairs, parts, near_blocks, received, hot, weights, low_left)
        if initial:
            partial = ordered(partial, returned)
        summed = exchange(partial.reshape(fem_count, share, local_rows), "fem")

        def fem_step(after):
            return fem_call(
                ordered(fem_state, after),
                fem_source,
                inverse,
                spread,
                returned,
                (*halos, others[0], others[2]),
                take,
                last,
            )

        if initial:
            spread, inverse = tables_call(ordered(codes, partial), reaction, excitations)
            summed = ordered(summed, spread)
        else:
            fem_state, *rest = fem_step(partial)
            summed = ordered(summed, fem_state)
        density, *more = update_call(
            summed, density, bem_source, diag_row, low_right, per_dev, last
        )
        if not last:
            copies, moment = more
        if initial:
            fem_state, *rest = fem_step(copies)
        if not last:
            values, *edges = rest
    return (fem_state, density)


def solution(mesh):
    return jax.shard_map(
        shards,
        mesh=mesh,
        in_specs=(
            P("fem", "bem", None, None),
            P("fem", "bem", None, None),
            P("fem", "bem", None),
            P(None, "bem"),
            P(None, "bem"),
            P("bem"),
            P("bem", "fem", None, None),
            P("bem", None),
            P("bem", None, None),
            P(),
            P(),
            P(("fem", "bem")),
            P(("fem", "bem"), None),
            P(("fem", "bem")),
        ),
        out_specs=(P("fem", "bem", None, None), P("fem", "bem")),
        check_vma=False,
    )
```
